32 devices in a mesh: gx: 4 (over y, core), gz: 4 (over z), grp: 2 (over x).
Axes of the slice: x: 2, y: 2, z: 4, core: 2. Of those that a mesh axis runs over, the one named last changes fastest.
Arguments:
- velocity: float32 [3, 3, 512, 2048], P(None, None, ('gz', 'grp'), 'gx'), may hold values from -5 to 5
- slab_average_downflow_speed: float32 [3], replicated, may hold values from 0.5 to 2
- mean_shear: float32 [3], replicated, may hold values from -2 to 2
- mode_counts: int32 [3, 2], replicated, may hold values from 64 to 128
Outputs:
- advanced: float32 [3, 3, 512, 2048], P(None, None, ('gz', 'grp'), 'gx')
- stress: float32 [6, 3, 512, 2048], P(None, None, ('gz', 'grp'), 'gx')
The draws below stay inside these ranges and needn't reach their ends.
All inputs are finite; a program needn't handle non-finite values.
Results may differ from the reference program's by a relative error of at most 0.00015.
Values sent between devices are 32-bit elements; how exact they have to be, the bound alone decides.
A program may use at most 64 MiB of HBM per device.

```python
import math
import jax
import jax.numpy as jnp
from jax import lax

NX = 2048
NZ = 512
MODES = 256
PLANES = 3


def band_table(length, half_modes):
    positions = jnp.arange(length, dtype=jnp.int32)
    numbers = jnp.arange(half_modes, dtype=jnp.int32) + 1
    phase_int = positions[:, None] * numbers[None, :] % length
    angles = phase_int.astype(jnp.float32) * jnp.float32(2.0 * math.pi / length)
    return jnp.concatenate([jnp.cos(angles), jnp.sin(angles)], axis=1)


def draw_velocity(key, part):
    first_key, second_key = jax.random.split(jax.random.fold_in(key, 7101))
    half_modes = MODES // 2
    amplitude = jax.random.normal(first_key, (3, PLANES, 2 * half_modes, 2 * half_modes), jnp.float32) / half_modes
    table_x = band_table(NX, half_modes)
    table_z = band_table(NZ, half_modes)
    partial_sum = jnp.einsum('cpnm,xm->cpnx', amplitude, table_x, precision=lax.Precision.HIGHEST)
    banded = jnp.einsum('zn,cpnx->cpzx', table_z, partial_sum, precision=lax.Precision.HIGHEST)
    rough_part = 0.5 * jax.random.normal(second_key, (3, PLANES, NZ, NX), jnp.float32)
    return jnp.clip(banded + rough_part, -5.0, 5.0)


def place_ends(drawn, own_key, smallest, top_value):
    place = [jax.random.randint(jax.random.fold_in(own_key, axis), (), 0, length) for axis, length in enumerate(drawn.shape)]
    main_axis = drawn.shape.index(max(drawn.shape))
    next_to = place[:main_axis] + [(place[main_axis] + 1) % drawn.shape[main_axis]] + place[main_axis + 1:]
    return drawn.at[tuple(place)].set(smallest).at[tuple(next_to)].set(top_value)


def setup_inputs(seed: int = 0) -> dict:
    splits = jax.random.split(jax.random.key(seed), 5)
    return {
        "velocity": draw_velocity(jax.random.fold_in(splits[4], 71), 0),
        "slab_average_downflow_speed": jnp.clip(jax.random.uniform(splits[1], (PLANES,), jnp.float32, 0.5, 2.0), 0.5, 2.0),
        "mean_shear": jnp.clip(jax.random.uniform(splits[2], (PLANES,), jnp.float32, -2.0, 2.0), -2.0, 2.0),
        "mode_counts": place_ends(jax.random.randint(splits[3], (PLANES, 2), MODES // 4, MODES // 2 + 1), jax.random.fold_in(splits[3], 1), MODES // 4, (MODES // 2 + 1) - 1).astype(jnp.int32),
    }


molecular_diffusivity = 0.4
time_step = 0.2
highest = lax.Precision.HIGHEST


def wave_numbers(modes):
    column = jnp.arange(modes, dtype=jnp.int32)
    half_modes = modes // 2
    return jnp.where(column < half_modes, column, column - half_modes + 1)


def wave_table(positions, length, modes):
    column = jnp.arange(modes, dtype=jnp.int32)
    numbers = wave_numbers(modes)
    phase_int = (positions[:, None] * numbers[None, :]) % length
    angles = phase_int.astype(jnp.float32) * jnp.float32(2.0 * math.pi / length)
    return jnp.where(column[None, :] < modes // 2, jnp.cos(angles), jnp.sin(angles))


def mode_weights(length, modes):
    column = jnp.arange(modes, dtype=jnp.int32)
    return jnp.where(column == 0, jnp.float32(1.0 / length), jnp.float32(2.0 / length))


def tendency_from(middle_entry, east_cells, west_cells, north_cells, south_cells, slab_average_downflow_speed, mean_shear):
    downflow_derivative_field = (east_cells - west_cells) * 0.5
    crossflow_derivative_field = (north_cells - south_cells) * 0.5
    diffusion_contribution = east_cells + west_cells + north_cells + south_cells - 4.0 * middle_entry
    holding_slab = slab_average_downflow_speed[:, None, None] + middle_entry[0]
    advanced_state = -holding_slab[None] * downflow_derivative_field - middle_entry[2][None] * crossflow_derivative_field + molecular_diffusivity * diffusion_contribution
    shear_term = mean_shear[:, None, None] * middle_entry[1]
    return jnp.concatenate([advanced_state[0:1] - shear_term[None], advanced_state[1:]], axis=0)


def runge_kutta(velocity, rate):
    first = velocity + time_step * rate(velocity)
    second = 0.75 * velocity + 0.25 * (first + time_step * rate(first))
    return velocity / 3.0 + (2.0 / 3.0) * (second + time_step * rate(second))


def reference(velocity, slab_average_downflow_speed, mean_shear, mode_counts):
    def rate(field):
        return tendency_from(field, jnp.roll(field, -1, axis=3), jnp.roll(field, 1, axis=3),
                             jnp.roll(field, -1, axis=2), jnp.roll(field, 1, axis=2), slab_average_downflow_speed, mean_shear)

    advanced = runge_kutta(velocity, rate)
    table_x = wave_table(jnp.arange(NX, dtype=jnp.int32), NX, MODES)
    table_z = wave_table(jnp.arange(NZ, dtype=jnp.int32), NZ, MODES)
    analysis_x = table_x * mode_weights(NX, MODES)[None, :]
    analysis_z = table_z * mode_weights(NZ, MODES)[None, :]
    numbers = wave_numbers(MODES)
    keep_z = numbers[None, :] <= mode_counts[:, 1][:, None]
    keep_x = numbers[None, :] <= mode_counts[:, 0][:, None]
    keep = (keep_z[:, :, None] & keep_x[:, None, :]).astype(jnp.float32)

    def filter_field(field):
        coeffs = jnp.einsum('pzx,xm->pzm', field, analysis_x, precision=highest)
        coeffs = jnp.einsum('pzm,zn->pnm', coeffs, analysis_z, precision=highest) * keep
        partial_sum = jnp.einsum('pnm,zn->pzm', coeffs, table_z, precision=highest)
        return jnp.einsum('pzm,xm->pzx', partial_sum, table_x, precision=highest)

    filtered_velocity = lax.map(filter_field, advanced)
    pair_first = jnp.array([0, 0, 0, 1, 1, 2], dtype=jnp.int32)
    pair_second = jnp.array([0, 1, 2, 1, 2, 2], dtype=jnp.int32)

    def one_stress(index):
        first_idx = pair_first[index]
        second_idx = pair_second[index]
        product = advanced[first_idx] * advanced[second_idx]
        return filter_field(product) - filtered_velocity[first_idx] * filtered_velocity[second_idx]

    stress = lax.map(one_stress, jnp.arange(6, dtype=jnp.int32))
    return advanced, stress
```

```python
import functools
import math

import jax
import jax.numpy as jnp
import numpy as np
from jax import lax
from jax.experimental import pallas as pl
from jax.experimental.pallas import tpu as pltpu
from jax.sharding import PartitionSpec as P

MODES = 256
FIELDS = 9
MESH = pl.DeviceIdType.MESH
ROWS = 8
LANES = 128

molecular_diffusivity = 0.4
time_step = 0.2
pair_first = (0, 0, 0, 1, 1, 2)
pair_second = (0, 1, 2, 1, 2, 2)
f32 = jnp.float32
bf16 = jnp.bfloat16


def wave_table(length):
    column = np.arange(MODES)
    half = MODES // 2
    numbers = np.where(column < half, column, column - half + 1)
    angles = (np.arange(length)[:, None] * numbers[None, :] % length) * (2.0 * math.pi / length)
    return np.where(column[None, :] < half, np.cos(angles), np.sin(angles)).astype(np.float32)


def split_table(table):
    high = table.astype(bf16)
    low = (table - high.astype(np.float32)).astype(bf16)
    return high, low


def split(values):
    high = values.astype(bf16)
    return high, (values - high.astype(f32)).astype(bf16)


def dot3(a, b, contract=((1,), (0,))):
    def one(x, y):
        return lax.dot_general(x, y, (contract, ((), ())), preferred_element_type=f32)

    return one(a[0], b[0]) + (one(a[0], b[1]) + one(a[1], b[0]))


def tendency_from(middle, east, west, north, south, slab, shear):
    downflow = (east - west) * 0.5
    crossflow = (north - south) * 0.5
    diffusion = east + west + north + south - 4.0 * middle
    holding = slab[:, None, None] + middle[0]
    state = (
        -holding[None] * downflow - middle[2][None] * crossflow + molecular_diffusivity * diffusion
    )
    return jnp.concatenate([state[0:1] - (shear[:, None, None] * middle[1])[None], state[1:]], axis=0)


def rate(padded, slab, shear):
    return tendency_from(
        padded[:, :, 1:-1, 1:-1],
        padded[:, :, 1:-1, 2:],
        padded[:, :, 1:-1, :-2],
        padded[:, :, 2:, 1:-1],
        padded[:, :, :-2, 1:-1],
        slab,
        shear,
    )


def inner(cells, width):
    return cells[:, :, width:-width, width:-width]


def runge_kutta(padded, slab, shear):
    first = inner(padded, 1) + time_step * rate(padded, slab, shear)
    second = 0.75 * inner(padded, 2) + 0.25 * (
        inner(first, 1) + time_step * rate(first, slab, shear)
    )
    return inner(padded, 3) / 3.0 + 2.0 / 3.0 * (
        inner(second, 1) + time_step * rate(second, slab, shear)
    )


def halo_kernel(sizes, v_ref, out_ref, send_sem, recv_sem, local_sem):
    gx_n, gz_n, grp_n = sizes
    z_n = gz_n * grp_n
    _, cz, cx = v_ref.shape
    gx = lax.axis_index("gx")
    z = lax.axis_index("gz") * grp_n + lax.axis_index("grp")
    steps = [(dx, dz) for dx in (-1, 0, 1) for dz in (-1, 0, 1) if dx or dz]

    def device(dx, dz):
        to_z = lax.rem(z + dz + z_n, z_n)
        return {
            "gx": lax.rem(gx + dx + gx_n, gx_n),
            "gz": lax.div(to_z, grp_n),
            "grp": lax.rem(to_z, grp_n),
        }

    barrier = pltpu.get_barrier_semaphore()
    for dx, dz in steps:
        pl.semaphore_signal(barrier, inc=1, device_id=device(dx, dz), device_id_type=MESH)
    pl.semaphore_wait(barrier, len(steps))
    source_x = {1: pl.ds(cx - LANES, LANES), -1: pl.ds(0, LANES), 0: pl.ds(0, cx)}
    target_x = {1: pl.ds(0, LANES), -1: pl.ds(LANES + cx, LANES), 0: pl.ds(LANES, cx)}
    source_z = {1: pl.ds(cz - ROWS, ROWS), -1: pl.ds(0, ROWS), 0: pl.ds(0, cz)}
    target_z = {1: pl.ds(0, ROWS), -1: pl.ds(ROWS + cz, ROWS), 0: pl.ds(ROWS, cz)}
    copies = []
    for index, (dx, dz) in enumerate(steps):
        copy = pltpu.make_async_remote_copy(
            src_ref=v_ref.at[:, source_z[dz], source_x[dx]],
            dst_ref=out_ref.at[:, target_z[dz], target_x[dx]],
            send_sem=send_sem.at[index],
            recv_sem=recv_sem.at[index],
            device_id=device(dx, dz),
            device_id_type=MESH,
        )
        copy.start()
        copies.append(copy)
    own = pltpu.make_async_copy(v_ref, out_ref.at[:, target_z[0], target_x[0]], local_sem)
    own.start()
    own.wait()
    for copy in copies:
        copy.wait()


def with_halo(velocity, sizes):
    count, cz, cx = velocity.shape
    return pl.pallas_call(
        functools.partial(halo_kernel, sizes),
        out_shape=jax.ShapeDtypeStruct((count, cz + 2 * ROWS, cx + 2 * LANES), f32),
        in_specs=[pl.BlockSpec(memory_space=pltpu.VMEM)],
        out_specs=pl.BlockSpec(memory_space=pl.ANY),
        scratch_shapes=[
            pltpu.SemaphoreType.DMA((8,)),
            pltpu.SemaphoreType.DMA((8,)),
            pltpu.SemaphoreType.DMA,
        ],
        compiler_params=pltpu.CompilerParams(collective_id=0, has_side_effects=True),
        name="halo",
    )(velocity)


def filter_kernel(
    sizes, planes, adv_ref, counts_ref, txh_hbm, txl_hbm, tzh_ref, tzl_ref, tth_ref, ttl_ref, out_ref,
    high, low, txh, txl, part_send, part_keep, part_recv, y_send, y_recv, z_send, z_recv, z_out, gath,
    table_sem, ps_sem, pr_sem, ys_sem, yr_sem, zs_sem, zr_sem, os_sem, gr_sem, gy_sem, gp_sem,
):
    gx_n, gz_n, grp_n = sizes
    z_n = gz_n * grp_n
    y_n = gx_n // 2
    units = gath.shape[0] // gx_n
    _, cz, cx = adv_ref.shape
    gx = lax.axis_index("gx")
    z = lax.axis_index("gz") * grp_n + lax.axis_index("grp")
    y, core = lax.div(gx, 2), lax.rem(gx, 2)
    other = 1 - core

    def at_x(to_y, to_core):
        return {"gx": 2 * to_y + to_core, "gz": lax.axis_index("gz"), "grp": lax.axis_index("grp")}

    def at_z(to_z):
        to_z = jnp.int32(to_z)
        return {"gx": gx, "gz": lax.div(to_z, grp_n), "grp": lax.rem(to_z, grp_n)}

    def remote(src, dst, send, recv, device):
        return pltpu.make_async_remote_copy(
            src_ref=src, dst_ref=dst, send_sem=send, recv_sem=recv, device_id=device, device_id_type=MESH
        )

    barrier = pltpu.get_barrier_semaphore()
    friends = [at_x(y, other)]
    friends += [at_x(lax.rem(y + d, y_n), core) for d in range(1, y_n)]
    friends += [at_z(lax.rem(z + d, z_n)) for d in range(1, z_n)]
    for friend in friends:
        pl.semaphore_signal(barrier, inc=1, device_id=friend, device_id_type=MESH)

    mine = pl.ds(pl.multiple_of(gx * cx, cx), cx)
    tables = [
        pltpu.make_async_copy(txh_hbm.at[mine, :], txh, table_sem.at[0]),
        pltpu.make_async_copy(txl_hbm.at[mine, :], txl, table_sem.at[1]),
    ]
    for copy in tables:
        copy.start()

    def put(unit, values):
        h, l = split(values)
        high[unit] = h
        low[unit] = l

    def prepare(p, carry):
        parts = [adv_ref[i * planes + p] for i in range(3)]
        for i in range(3):
            put(p * FIELDS + i, parts[i])
        for q, (a, b) in enumerate(zip(pair_first, pair_second)):
            put(p * FIELDS + 3 + q, parts[a] * parts[b])
        return carry

    lax.fori_loop(0, planes, prepare, 0)
    for unit in range(planes * FIELDS, gath.shape[0]):
        high[unit] = jnp.zeros((cz, cx), bf16)
        low[unit] = jnp.zeros((cz, cx), bf16)
    for copy in tables:
        copy.wait()
    pl.semaphore_wait(barrier, len(friends))

    def analyse(block):
        chosen = pl.ds(block * units, units)
        rows = (high[chosen].reshape(units * cz, cx), low[chosen].reshape(units * cz, cx))
        return dot3(rows, (txh[...], txl[...])).reshape(units, cz, MODES)

    order = list(range(1, y_n)) + [0]
    to_partner = [
        remote(part_send.at[d], part_recv.at[d], ps_sem.at[d], pr_sem.at[d], at_x(y, other))
        for d in range(y_n)
    ]
    for d in order:
        part_send[d] = analyse(2 * lax.rem(y + d, y_n) + other)
        to_partner[d].start()
    for d in order:
        part_keep[d] = analyse(2 * lax.rem(y + d, y_n) + core)
    to_y = {
        d: remote(
            y_send.at[d - 1], y_recv.at[d - 1], ys_sem.at[d - 1], yr_sem.at[d - 1],
            at_x(lax.rem(y + d, y_n), core),
        )
        for d in range(1, y_n)
    }
    for d in range(1, y_n):
        to_partner[d].wait_recv()
        y_send[d - 1] = part_keep[d] + part_recv[d]
        to_y[d].start()
    to_partner[0].wait_recv()
    for d in range(1, y_n):
        to_y[d].wait_recv()

    def forward(k, device_slot):
        return remote(z_send.at[k], z_recv.at[z], zs_sem.at[k], zr_sem.at[device_slot], at_z(k))

    for k in range(units):
        total = part_keep[0, k] + part_recv[0, k]
        for d in range(1, y_n):
            total = total + y_recv[d - 1, k]
        z_send[k] = total

        @pl.when(z != k)
        def _():
            forward(k, z).start()

        @pl.when(z == k)
        def _():
            z_recv[z] = total

    unit = gx * units + z

    def back(s, slot):
        return remote(z_out.at[s], gath.at[slot], os_sem.at[s], gr_sem.at[slot], at_z(s))

    @pl.when(z < units)
    def _():
        for s in range(z_n):

            @pl.when(z != s)
            def _():
                remote(z_send.at[0], z_recv.at[s], zs_sem.at[0], zr_sem.at[s], at_z(s)).wait_recv()

        plane = jnp.minimum(lax.div(unit, FIELDS), planes - 1)
        limit_x, limit_z = counts_ref[plane, 0], counts_ref[plane, 1]

        def numbers(axis):
            column = lax.broadcasted_iota(jnp.int32, (MODES, MODES), axis)
            half = MODES // 2
            return jnp.where(column < half, column, column - half + 1), column

        def weights(column, length):
            return jnp.where(column == 0, f32(1.0 / length), f32(2.0 / length))

        kz, nz = numbers(0)
        kx, nx = numbers(1)
        scale = weights(nz, z_n * cz) * weights(nx, gx_n * cx)
        scale = jnp.where((kz <= limit_z) & (kx <= limit_x), scale, 0.0)
        lines = split(z_recv[...].reshape(z_n * cz, MODES))
        spectral = dot3((tth_ref[...], ttl_ref[...]), lines) * scale
        z_out[...] = dot3((tzh_ref[...], tzl_ref[...]), split(spectral)).reshape(z_n, cz, MODES)
        for s in range(z_n):

            @pl.when(z != s)
            def _():
                back(s, unit).start()

            @pl.when(z == s)
            def _():
                gath[unit] = z_out[s]

    def spread(slot, k, d):
        return remote(
            gath.at[slot], gath.at[slot], gy_sem.at[d - 1, k], gr_sem.at[slot],
            at_x(lax.rem(y + d, y_n), core),
        )

    def share(slot, d, k):
        return remote(gath.at[slot], gath.at[slot], gp_sem.at[d, k], gr_sem.at[slot], at_x(y, other))

    for k in range(units):
        slot = gx * units + k

        @pl.when(z != k)
        def _():
            back(0, slot).wait_recv()

        for d in range(1, y_n):
            spread(slot, k, d).start()
        share(slot, 0, k).start()
    for d in range(1, y_n):
        for k in range(units):
            slot = (2 * lax.rem(y + d, y_n) + core) * units + k
            back(0, slot).wait_recv()
            share(slot, d, k).start()
    for d in range(y_n):
        for k in range(units):
            back(0, (2 * lax.rem(y + d, y_n) + other) * units + k).wait_recv()

    def synthesise(p, carry):
        rows = split(gath[pl.ds(p * FIELDS, FIELDS)].reshape(FIELDS * cz, MODES))
        filtered = dot3(rows, (txh[...], txl[...]), ((1,), (1,))).reshape(FIELDS, cz, cx)
        for q, (a, b) in enumerate(zip(pair_first, pair_second)):
            out_ref[q * planes + p] = filtered[3 + q] - filtered[a] * filtered[b]
        return carry

    lax.fori_loop(0, planes, synthesise, 0)

    for d in range(y_n):
        to_partner[d].wait_send()
    for d in range(1, y_n):
        to_y[d].wait_send()
    for k in range(units):

        @pl.when(z != k)
        def _():
            forward(k, z).wait_send()

        for d in range(1, y_n):
            spread(gx * units + k, k, d).wait_send()
        for d in range(y_n):
            share(gx * units + k, d, k).wait_send()

    @pl.when(z < units)
    def _():
        for s in range(z_n):

            @pl.when(z != s)
            def _():
                back(s, unit).wait_send()


def filtered_stress(advanced, mode_counts, sizes):
    gx_n, gz_n, grp_n = sizes
    z_n = gz_n * grp_n
    y_n = gx_n // 2
    count, cz, cx = advanced.shape
    planes = count // 3
    units = -(-FIELDS * planes // gx_n)
    assert gx_n % 2 == 0 and units <= z_n
    txh, txl = split_table(wave_table(cx * gx_n))
    table_z = wave_table(cz * z_n)
    tzh, tzl = split_table(table_z)
    tth, ttl = split_table(table_z.T)
    dma = pltpu.SemaphoreType.DMA
    vmem = pl.BlockSpec(memory_space=pltpu.VMEM)
    anywhere = pl.BlockSpec(memory_space=pl.ANY)
    others = max(y_n - 1, 1)
    total = gx_n * units
    return pl.pallas_call(
        functools.partial(filter_kernel, sizes, planes),
        out_shape=jax.ShapeDtypeStruct((6 * planes, cz, cx), f32),
        in_specs=[vmem, pl.BlockSpec(memory_space=pltpu.SMEM), anywhere, anywhere, vmem, vmem, vmem, vmem],
        out_specs=vmem,
        scratch_shapes=[
            pltpu.VMEM((total, cz, cx), bf16),
            pltpu.VMEM((total, cz, cx), bf16),
            pltpu.VMEM((cx, MODES), bf16),
            pltpu.VMEM((cx, MODES), bf16),
            pltpu.VMEM((y_n, units, cz, MODES), f32),
            pltpu.VMEM((y_n, units, cz, MODES), f32),
            pltpu.VMEM((y_n, units, cz, MODES), f32),
            pltpu.VMEM((others, units, cz, MODES), f32),
            pltpu.VMEM((others, units, cz, MODES), f32),
            pltpu.VMEM((units, cz, MODES), f32),
            pltpu.VMEM((z_n, cz, MODES), f32),
            pltpu.VMEM((z_n, cz, MODES), f32),
            pltpu.VMEM((total, cz, MODES), f32),
            dma((2,)),
            dma((y_n,)),
            dma((y_n,)),
            dma((others,)),
            dma((others,)),
            dma((units,)),
            dma((z_n,)),
            dma((z_n,)),
            dma((total,)),
            dma((others, units)),
            dma((y_n, units)),
        ],
        compiler_params=pltpu.CompilerParams(collective_id=1, has_side_effects=True),
        name="filter",
    )(advanced, mode_counts, *(jnp.asarray(t) for t in (txh, txl, tzh, tzl, tth, ttl)))


def local(sizes, velocity, slab, shear, mode_counts):
    three, planes, cz, cx = velocity.shape
    padded = with_halo(velocity.reshape(three * planes, cz, cx), sizes)
    padded = padded.reshape(three, planes, cz + 2 * ROWS, cx + 2 * LANES)
    padded = padded[:, :, ROWS - 3 : ROWS + cz + 3, LANES - 3 : LANES + cx + 3]
    advanced = runge_kutta(padded, slab, shear)
    stress = filtered_stress(advanced.reshape(three * planes, cz, cx), mode_counts, sizes)
    return advanced, stress.reshape(6, planes, cz, cx)


def solution(mesh):
    sizes = (mesh.shape["gx"], mesh.shape["gz"], mesh.shape["grp"])
    spread = P(None, None, ("gz", "grp"), "gx")
    return jax.shard_map(
        functools.partial(local, sizes),
        mesh=mesh,
        in_specs=(spread, P(), P(), P()),
        out_specs=(spread, spread),
        check_vma=False,
    )
```

```python
import functools
import math

import jax
import jax.numpy as jnp
import numpy as np
from jax import lax
from jax.experimental import pallas as pl
from jax.experimental.pallas import tpu as pltpu
from jax.sharding import PartitionSpec as P

MODES = 256
FIELDS = 9
MESH = pl.DeviceIdType.MESH
ROWS = 8
LANES = 128

molecular_diffusivity = 0.4
time_step = 0.2
pair_first = (0, 0, 0, 1, 1, 2)
pair_second = (0, 1, 2, 1, 2, 2)
f32 = jnp.float32
bf16 = jnp.bfloat16


def wave_table(length):
    column = np.arange(MODES)
    half = MODES // 2
    numbers = np.where(column < half, column, column - half + 1)
    angles = (np.arange(length)[:, None] * numbers[None, :] % length) * (2.0 * math.pi / length)
    return np.where(column[None, :] < half, np.cos(angles), np.sin(angles)).astype(np.float32)


def split_table(table):
    high = table.astype(bf16)
    low = (table - high.astype(np.float32)).astype(bf16)
    return high, low


def split(values):
    high = values.astype(bf16)
    return high, (values - high.astype(f32)).astype(bf16)


def dot3(a, b, contract=((1,), (0,))):
    def one(x, y):
        return lax.dot_general(x, y, (contract, ((), ())), preferred_element_type=f32)

    return one(a[0], b[0]) + (one(a[0], b[1]) + one(a[1], b[0]))


def halo_kernel(sizes, v_ref, zh_ref, xh_ref, corner_ref, strips, send_sem, recv_sem):
    gx_n, gz_n, grp_n = sizes
    z_n = gz_n * grp_n
    count, cz, cx = v_ref.shape
    gx = lax.axis_index("gx")
    z = lax.axis_index("gz") * grp_n + lax.axis_index("grp")
    steps = [(dx, dz) for dx in (-1, 0, 1) for dz in (-1, 0, 1) if dx or dz]

    def device(dx, dz):
        to_z = lax.rem(z + dz + z_n, z_n)
        return {
            "gx": lax.rem(gx + dx + gx_n, gx_n),
            "gz": lax.div(to_z, grp_n),
            "grp": lax.rem(to_z, grp_n),
        }

    barrier = pltpu.get_barrier_semaphore()
    for dx, dz in steps:
        pl.semaphore_signal(barrier, inc=1, device_id=device(dx, dz), device_id_type=MESH)
    for c in range(count):
        strips[0, c] = v_ref[c, :, 0:LANES].T[0:ROWS]
        strips[1, c] = v_ref[c, :, cx - LANES : cx].T[LANES - ROWS : LANES]
    pl.semaphore_wait(barrier, len(steps))
    edge_x = {1: pl.ds(cx - LANES, LANES), -1: pl.ds(0, LANES), 0: pl.ds(0, cx)}
    edge_z = {1: pl.ds(cz - ROWS, ROWS), -1: pl.ds(0, ROWS)}
    copies = []
    for index, (dx, dz) in enumerate(steps):
        side_x, side_z = int(dx > 0), int(dz > 0)
        if dz == 0:
            source, target = strips.at[side_x], xh_ref.at[side_x]
        else:
            source = v_ref.at[:, edge_z[dz], edge_x[dx]]
            target = zh_ref.at[side_z] if dx == 0 else corner_ref.at[2 * side_z + side_x]
        copies.append(
            pltpu.make_async_remote_copy(
                src_ref=source,
                dst_ref=target,
                send_sem=send_sem.at[index],
                recv_sem=recv_sem.at[index],
                device_id=device(dx, dz),
                device_id_type=MESH,
            )
        )
    for copy in copies:
        copy.start()
    for copy in copies:
        copy.wait()


def halos(velocity, sizes):
    count, cz, cx = velocity.shape
    vmem = pl.BlockSpec(memory_space=pltpu.VMEM)
    return pl.pallas_call(
        functools.partial(halo_kernel, sizes),
        out_shape=(
            jax.ShapeDtypeStruct((2, count, ROWS, cx), f32),
            jax.ShapeDtypeStruct((2, count, ROWS, cz), f32),
            jax.ShapeDtypeStruct((4, count, ROWS, LANES), f32),
        ),
        in_specs=[vmem],
        out_specs=(vmem, vmem, vmem),
        scratch_shapes=[
            pltpu.VMEM((2, count, ROWS, cz), f32),
            pltpu.SemaphoreType.DMA((8,)),
            pltpu.SemaphoreType.DMA((8,)),
        ],
        compiler_params=pltpu.CompilerParams(collective_id=0, has_side_effects=True),
        name="halo",
    )(velocity)


def step_kernel(v_ref, zh_ref, xh_ref, corner_ref, slab_ref, shear_ref, out_ref, start, first, second):
    p = pl.program_id(0)
    slab, shear = slab_ref[p], shear_ref[p]
    _, _, cz, cx = v_ref.shape
    top = 2 * ROWS
    lane = lax.broadcasted_iota(jnp.int32, (ROWS, LANES), 1)
    width = cx + LANES
    for c in range(3):
        start[c, top : top + cz, 0:cx] = v_ref[c, 0]
        strip = jnp.concatenate(
            [xh_ref[0, c, 0], jnp.zeros((LANES - 2 * ROWS, cz), f32), xh_ref[1, c, 0]], axis=0
        )
        start[c, top : top + cz, cx:width] = strip.T
        for side, row in ((1, top - ROWS), (0, top + cz)):
            start[c, row : row + ROWS, 0:cx] = zh_ref[side, c, 0]
            start[c, row : row + ROWS, cx:width] = jnp.where(
                lane < LANES // 2, corner_ref[2 * side, c, 0], corner_ref[2 * side + 1, c, 0]
            )

    def block(source, row):
        middle = [source[c, row : row + ROWS, :] for c in range(3)]
        rates = []
        for c in range(3):
            north = source[c, row + 1 : row + 1 + ROWS, :]
            south = source[c, row - 1 : row - 1 + ROWS, :]
            east = pltpu.roll(middle[c], width - 1, 1)
            west = pltpu.roll(middle[c], 1, 1)
            value = (
                -(slab + middle[0]) * ((east - west) * 0.5)
                - middle[2] * ((north - south) * 0.5)
                + molecular_diffusivity * (east + west + north + south - 4.0 * middle[c])
            )
            rates.append(value - shear * middle[1] if c == 0 else value)
        return middle, rates

    for row in range(ROWS, top + cz + ROWS, ROWS):
        middle, rates = block(start, row)
        for c in range(3):
            first[c, row : row + ROWS, :] = middle[c] + time_step * rates[c]
    for row in range(ROWS, top + cz + ROWS, ROWS):
        middle, rates = block(first, row)
        for c in range(3):
            second[c, row : row + ROWS, :] = 0.75 * start[c, row : row + ROWS, :] + 0.25 * (
                middle[c] + time_step * rates[c]
            )
    for row in range(top, top + cz, ROWS):
        middle, rates = block(second, row)
        for c in range(3):
            value = start[c, row : row + ROWS, :] * (1.0 / 3.0) + (2.0 / 3.0) * (
                middle[c] + time_step * rates[c]
            )
            out_ref[c, 0, row - top : row - top + ROWS, :] = value[:, 0:cx]


def advance(velocity, slab, shear, sizes):
    three, planes, cz, cx = velocity.shape
    zh, xh, corner = halos(velocity.reshape(three * planes, cz, cx), sizes)
    smem = pl.BlockSpec(memory_space=pltpu.SMEM)
    main = pl.BlockSpec((3, 1, cz, cx), lambda p: (0, p, 0, 0))

    def edge(sides, lanes):
        return pl.BlockSpec((sides, 3, 1, ROWS, lanes), lambda p: (0, 0, p, 0, 0))

    return pl.pallas_call(
        step_kernel,
        grid=(planes,),
        out_shape=jax.ShapeDtypeStruct(velocity.shape, f32),
        in_specs=[main, edge(2, cx), edge(2, cz), edge(4, LANES), smem, smem],
        out_specs=main,
        scratch_shapes=[pltpu.VMEM((3, cz + 4 * ROWS, cx + LANES), f32)] * 3,
        name="step",
    )(
        velocity,
        zh.reshape(2, three, planes, ROWS, cx),
        xh.reshape(2, three, planes, ROWS, cz),
        corner.reshape(4, three, planes, ROWS, LANES),
        slab,
        shear,
    )


def filter_kernel(
    sizes, planes, adv_ref, counts_ref, txh_hbm, txl_hbm, tzh_ref, tzl_ref, tth_ref, ttl_ref, out_ref,
    high, low, txh, txl, part_send, part_keep, part_recv, y_send, y_recv, z_send, z_recv, z_out, gath,
    table_sem, ps_sem, pr_sem, ys_sem, yr_sem, zs_sem, zr_sem, os_sem, gr_sem, gy_sem, gp_sem,
):
    gx_n, gz_n, grp_n = sizes
    z_n = gz_n * grp_n
    y_n = gx_n // 2
    units = gath.shape[0] // gx_n
    _, cz, cx = adv_ref.shape
    gx = lax.axis_index("gx")
    z = lax.axis_index("gz") * grp_n + lax.axis_index("grp")
    y, core = lax.div(gx, 2), lax.rem(gx, 2)
    other = 1 - core

    def at_x(to_y, to_core):
        return {"gx": 2 * to_y + to_core, "gz": lax.axis_index("gz"), "grp": lax.axis_index("grp")}

    def at_z(to_z):
        to_z = jnp.int32(to_z)
        return {"gx": gx, "gz": lax.div(to_z, grp_n), "grp": lax.rem(to_z, grp_n)}

    def remote(src, dst, send, recv, device):
        return pltpu.make_async_remote_copy(
            src_ref=src, dst_ref=dst, send_sem=send, recv_sem=recv, device_id=device, device_id_type=MESH
        )

    barrier = pltpu.get_barrier_semaphore()
    friends = [at_x(y, other)]
    friends += [at_x(lax.rem(y + d, y_n), core) for d in range(1, y_n)]
    friends += [at_z(lax.rem(z + d, z_n)) for d in range(1, z_n)]
    for friend in friends:
        pl.semaphore_signal(barrier, inc=1, device_id=friend, device_id_type=MESH)

    mine = pl.ds(pl.multiple_of(gx * cx, cx), cx)
    tables = [
        pltpu.make_async_copy(txh_hbm.at[mine, :], txh, table_sem.at[0]),
        pltpu.make_async_copy(txl_hbm.at[mine, :], txl, table_sem.at[1]),
    ]
    for copy in tables:
        copy.start()

    def put(unit, values):
        h, l = split(values)
        high[unit] = h
        low[unit] = l

    def prepare(p, carry):
        parts = [adv_ref[i * planes + p] for i in range(3)]
        for i in range(3):
            put(p * FIELDS + i, parts[i])
        for q, (a, b) in enumerate(zip(pair_first, pair_second)):
            put(p * FIELDS + 3 + q, parts[a] * parts[b])
        return carry

    lax.fori_loop(0, planes, prepare, 0)
    for unit in range(planes * FIELDS, gath.shape[0]):
        high[unit] = jnp.zeros((cz, cx), bf16)
        low[unit] = jnp.zeros((cz, cx), bf16)
    for copy in tables:
        copy.wait()
    pl.semaphore_wait(barrier, len(friends))

    def analyse(block):
        chosen = pl.ds(block * units, units)
        rows = (high[chosen].reshape(units * cz, cx), low[chosen].reshape(units * cz, cx))
        return dot3(rows, (txh[...], txl[...])).reshape(units, cz, MODES)

    order = list(range(1, y_n)) + [0]
    to_partner = [
        remote(part_send.at[d], part_recv.at[d], ps_sem.at[d], pr_sem.at[d], at_x(y, other))
        for d in range(y_n)
    ]
    for d in order:
        part_send[d] = analyse(2 * lax.rem(y + d, y_n) + other)
        to_partner[d].start()
    for d in order:
        part_keep[d] = analyse(2 * lax.rem(y + d, y_n) + core)
    to_y = {
        d: remote(
            y_send.at[d - 1], y_recv.at[d - 1], ys_sem.at[d - 1], yr_sem.at[d - 1],
            at_x(lax.rem(y + d, y_n), core),
        )
        for d in range(1, y_n)
    }
    for d in range(1, y_n):
        to_partner[d].wait_recv()
        y_send[d - 1] = part_keep[d] + part_recv[d]
        to_y[d].start()
    to_partner[0].wait_recv()
    for d in range(1, y_n):
        to_y[d].wait_recv()

    def forward(k, device_slot):
        return remote(z_send.at[k], z_recv.at[z], zs_sem.at[k], zr_sem.at[device_slot], at_z(k))

    for k in range(units):
        total = part_keep[0, k] + part_recv[0, k]
        for d in range(1, y_n):
            total = total + y_recv[d - 1, k]
        z_send[k] = total

        @pl.when(z != k)
        def _():
            forward(k, z).start()

        @pl.when(z == k)
        def _():
            z_recv[z] = total

    unit = gx * units + z

    def back(s, slot):
        return remote(z_out.at[s], gath.at[slot], os_sem.at[s], gr_sem.at[slot], at_z(s))

    @pl.when(z < units)
    def _():
        for s in range(z_n):

            @pl.when(z != s)
            def _():
                remote(z_send.at[0], z_recv.at[s], zs_sem.at[0], zr_sem.at[s], at_z(s)).wait_recv()

        plane = jnp.minimum(lax.div(unit, FIELDS), planes - 1)
        limit_x, limit_z = counts_ref[plane, 0], counts_ref[plane, 1]

        def numbers(axis):
            column = lax.broadcasted_iota(jnp.int32, (MODES, MODES), axis)
            half = MODES // 2
            return jnp.where(column < half, column, column - half + 1), column

        def weights(column, length):
            return jnp.where(column == 0, f32(1.0 / length), f32(2.0 / length))

        kz, nz = numbers(0)
        kx, nx = numbers(1)
        scale = weights(nz, z_n * cz) * weights(nx, gx_n * cx)
        scale = jnp.where((kz <= limit_z) & (kx <= limit_x), scale, 0.0)
        lines = split(z_recv[...].reshape(z_n * cz, MODES))
        spectral = dot3((tth_ref[...], ttl_ref[...]), lines) * scale
        z_out[...] = dot3((tzh_ref[...], tzl_ref[...]), split(spectral)).reshape(z_n, cz, MODES)
        for s in range(z_n):

            @pl.when(z != s)
            def _():
                back(s, unit).start()

            @pl.when(z == s)
            def _():
                gath[unit] = z_out[s]

    def spread(slot, k, d):
        return remote(
            gath.at[slot], gath.at[slot], gy_sem.at[d - 1, k], gr_sem.at[slot],
            at_x(lax.rem(y + d, y_n), core),
        )

    def share(slot, d, k):
        return remote(gath.at[slot], gath.at[slot], gp_sem.at[d, k], gr_sem.at[slot], at_x(y, other))

    for k in range(units):
        slot = gx * units + k

        @pl.when(z != k)
        def _():
            back(0, slot).wait_recv()

        for d in range(1, y_n):
            spread(slot, k, d).start()
        share(slot, 0, k).start()
    for d in range(1, y_n):
        for k in range(units):
            slot = (2 * lax.rem(y + d, y_n) + core) * units + k
            back(0, slot).wait_recv()
            share(slot, d, k).start()
    for d in range(y_n):
        for k in range(units):
            back(0, (2 * lax.rem(y + d, y_n) + other) * units + k).wait_recv()

    def synthesise(p, carry):
        rows = split(gath[pl.ds(p * FIELDS, FIELDS)].reshape(FIELDS * cz, MODES))
        filtered = dot3(rows, (txh[...], txl[...]), ((1,), (1,))).reshape(FIELDS, cz, cx)
        for q, (a, b) in enumerate(zip(pair_first, pair_second)):
            out_ref[q * planes + p] = filtered[3 + q] - filtered[a] * filtered[b]
        return carry

    lax.fori_loop(0, planes, synthesise, 0)

    for d in range(y_n):
        to_partner[d].wait_send()
    for d in range(1, y_n):
        to_y[d].wait_send()
    for k in range(units):

        @pl.when(z != k)
        def _():
            forward(k, z).wait_send()

        for d in range(1, y_n):
            spread(gx * units + k, k, d).wait_send()
        for d in range(y_n):
            share(gx * units + k, d, k).wait_send()

    @pl.when(z < units)
    def _():
        for s in range(z_n):

            @pl.when(z != s)
            def _():
                back(s, unit).wait_send()


def filtered_stress(advanced, mode_counts, sizes):
    gx_n, gz_n, grp_n = sizes
    z_n = gz_n * grp_n
    y_n = gx_n // 2
    count, cz, cx = advanced.shape
    planes = count // 3
    units = -(-FIELDS * planes // gx_n)
    assert gx_n % 2 == 0 and units <= z_n
    txh, txl = split_table(wave_table(cx * gx_n))
    table_z = wave_table(cz * z_n)
    tzh, tzl = split_table(table_z)
    tth, ttl = split_table(table_z.T)
    dma = pltpu.SemaphoreType.DMA
    vmem = pl.BlockSpec(memory_space=pltpu.VMEM)
    anywhere = pl.BlockSpec(memory_space=pl.ANY)
    others = max(y_n - 1, 1)
    total = gx_n * units
    return pl.pallas_call(
        functools.partial(filter_kernel, sizes, planes),
        out_shape=jax.ShapeDtypeStruct((6 * planes, cz, cx), f32),
        in_specs=[vmem, pl.BlockSpec(memory_space=pltpu.SMEM), anywhere, anywhere, vmem, vmem, vmem, vmem],
        out_specs=vmem,
        scratch_shapes=[
            pltpu.VMEM((total, cz, cx), bf16),
            pltpu.VMEM((total, cz, cx), bf16),
            pltpu.VMEM((cx, MODES), bf16),
            pltpu.VMEM((cx, MODES), bf16),
            pltpu.VMEM((y_n, units, cz, MODES), f32),
            pltpu.VMEM((y_n, units, cz, MODES), f32),
            pltpu.VMEM((y_n, units, cz, MODES), f32),
            pltpu.VMEM((others, units, cz, MODES), f32),
            pltpu.VMEM((others, units, cz, MODES), f32),
            pltpu.VMEM((units, cz, MODES), f32),
            pltpu.VMEM((z_n, cz, MODES), f32),
            pltpu.VMEM((z_n, cz, MODES), f32),
            pltpu.VMEM((total, cz, MODES), f32),
            dma((2,)),
            dma((y_n,)),
            dma((y_n,)),
            dma((others,)),
            dma((others,)),
            dma((units,)),
            dma((z_n,)),
            dma((z_n,)),
            dma((total,)),
            dma((others, units)),
            dma((y_n, units)),
        ],
        compiler_params=pltpu.CompilerParams(collective_id=1, has_side_effects=True),
        name="filter",
    )(advanced, mode_counts, *(jnp.asarray(t) for t in (txh, txl, tzh, tzl, tth, ttl)))


def local(sizes, velocity, slab, shear, mode_counts):
    three, planes, cz, cx = velocity.shape
    advanced = advance(velocity, slab, shear, sizes)
    stress = filtered_stress(advanced.reshape(three * planes, cz, cx), mode_counts, sizes)
    return advanced, stress.reshape(6, planes, cz, cx)


def solution(mesh):
    sizes = (mesh.shape["gx"], mesh.shape["gz"], mesh.shape["grp"])
    spread = P(None, None, ("gz", "grp"), "gx")
    return jax.shard_map(
        functools.partial(local, sizes),
        mesh=mesh,
        in_specs=(spread, P(), P(), P()),
        out_specs=(spread, spread),
        check_vma=False,
    )
```

```python
import functools
import math

import jax
import jax.numpy as jnp
import numpy as np
from jax import lax
from jax.experimental import pallas as pl
from jax.experimental.pallas import tpu as pltpu
from jax.sharding import PartitionSpec as P

MODES = 256
FIELDS = 9
MESH = pl.DeviceIdType.MESH
ROWS = 8
LANES = 128

molecular_diffusivity = 0.4
time_step = 0.2
pair_first = (0, 0, 0, 1, 1, 2)
pair_second = (0, 1, 2, 1, 2, 2)
f32 = jnp.float32
bf16 = jnp.bfloat16


def wave_table(length):
    column = np.arange(MODES)
    half = MODES // 2
    numbers = np.where(column < half, column, column - half + 1)
    angles = (np.arange(length)[:, None] * numbers[None, :] % length) * (2.0 * math.pi / length)
    return np.where(column[None, :] < half, np.cos(angles), np.sin(angles)).astype(np.float32)


def split_table(table):
    high = table.astype(bf16)
    low = (table - high.astype(np.float32)).astype(bf16)
    return high, low


def split(values):
    high = values.astype(bf16)
    return high, (values - high.astype(f32)).astype(bf16)


def dot3(a, b, contract=((1,), (0,))):
    def one(x, y):
        return lax.dot_general(x, y, (contract, ((), ())), preferred_element_type=f32)

    return one(a[0], b[0]) + (one(a[0], b[1]) + one(a[1], b[0]))


def halo_kernel(sizes, v_ref, zh_ref, xh_ref, corner_ref, strips, send_sem, recv_sem):
    gx_n, gz_n, grp_n = sizes
    z_n = gz_n * grp_n
    count, cz, cx = v_ref.shape
    gx = lax.axis_index("gx")
    z = lax.axis_index("gz") * grp_n + lax.axis_index("grp")
    steps = [(dx, dz) for dx in (-1, 0, 1) for dz in (-1, 0, 1) if dx or dz]

    def device(dx, dz):
        to_z = lax.rem(z + dz + z_n, z_n)
        return {
            "gx": lax.rem(gx + dx + gx_n, gx_n),
            "gz": lax.div(to_z, grp_n),
            "grp": lax.rem(to_z, grp_n),
        }

    barrier = pltpu.get_barrier_semaphore()
    for dx, dz in steps:
        pl.semaphore_signal(barrier, inc=1, device_id=device(dx, dz), device_id_type=MESH)
    for c in range(count):
        strips[0, c] = v_ref[c, :, 0:LANES].T[0:ROWS]
        strips[1, c] = v_ref[c, :, cx - LANES : cx].T[LANES - ROWS : LANES]
    pl.semaphore_wait(barrier, len(steps))
    edge_x = {1: pl.ds(cx - LANES, LANES), -1: pl.ds(0, LANES), 0: pl.ds(0, cx)}
    edge_z = {1: pl.ds(cz - ROWS, ROWS), -1: pl.ds(0, ROWS)}
    copies = []
    for index, (dx, dz) in enumerate(steps):
        side_x, side_z = int(dx > 0), int(dz > 0)
        if dz == 0:
            source, target = strips.at[side_x], xh_ref.at[side_x]
        else:
            source = v_ref.at[:, edge_z[dz], edge_x[dx]]
            target = zh_ref.at[side_z] if dx == 0 else corner_ref.at[2 * side_z + side_x]
        copies.append(
            pltpu.make_async_remote_copy(
                src_ref=source,
                dst_ref=target,
                send_sem=send_sem.at[index],
                recv_sem=recv_sem.at[index],
                device_id=device(dx, dz),
                device_id_type=MESH,
            )
        )
    for copy in copies:
        copy.start()
    for copy in copies:
        copy.wait()


def halos(velocity, sizes):
    count, cz, cx = velocity.shape
    vmem = pl.BlockSpec(memory_space=pltpu.VMEM)
    return pl.pallas_call(
        functools.partial(halo_kernel, sizes),
        out_shape=(
            jax.ShapeDtypeStruct((2, count, ROWS, cx), f32),
            jax.ShapeDtypeStruct((2, count, ROWS, cz), f32),
            jax.ShapeDtypeStruct((4, count, ROWS, LANES), f32),
        ),
        in_specs=[vmem],
        out_specs=(vmem, vmem, vmem),
        scratch_shapes=[
            pltpu.VMEM((2, count, ROWS, cz), f32),
            pltpu.SemaphoreType.DMA((8,)),
            pltpu.SemaphoreType.DMA((8,)),
        ],
        compiler_params=pltpu.CompilerParams(collective_id=0, has_side_effects=True),
        name="halo",
    )(velocity)


def step_kernel(v_ref, zh_ref, xh_ref, corner_ref, slab_ref, shear_ref, out_ref, start, first, second):
    p = pl.program_id(0)
    slab, shear = slab_ref[p], shear_ref[p]
    _, _, cz, cx = v_ref.shape
    top = 2 * ROWS
    lane = lax.broadcasted_iota(jnp.int32, (ROWS, LANES), 1)
    width = cx + LANES
    for c in range(3):
        start[c, top : top + cz, 0:cx] = v_ref[c, 0]
        strip = jnp.concatenate(
            [xh_ref[0, c, 0], jnp.zeros((LANES - 2 * ROWS, cz), f32), xh_ref[1, c, 0]], axis=0
        )
        start[c, top : top + cz, cx:width] = strip.T
        for side, row in ((1, top - ROWS), (0, top + cz)):
            start[c, row : row + ROWS, 0:cx] = zh_ref[side, c, 0]
            start[c, row : row + ROWS, cx:width] = jnp.where(
                lane < LANES // 2, corner_ref[2 * side, c, 0], corner_ref[2 * side + 1, c, 0]
            )

    def block(source, row):
        middle = [source[c, row : row + ROWS, :] for c in range(3)]
        rates = []
        for c in range(3):
            north = source[c, row + 1 : row + 1 + ROWS, :]
            south = source[c, row - 1 : row - 1 + ROWS, :]
            east = pltpu.roll(middle[c], width - 1, 1)
            west = pltpu.roll(middle[c], 1, 1)
            value = (
                -(slab + middle[0]) * ((east - west) * 0.5)
                - middle[2] * ((north - south) * 0.5)
                + molecular_diffusivity * (east + west + north + south - 4.0 * middle[c])
            )
            rates.append(value - shear * middle[1] if c == 0 else value)
        return middle, rates

    for row in range(ROWS, top + cz + ROWS, ROWS):
        middle, rates = block(start, row)
        for c in range(3):
            first[c, row : row + ROWS, :] = middle[c] + time_step * rates[c]
    for row in range(ROWS, top + cz + ROWS, ROWS):
        middle, rates = block(first, row)
        for c in range(3):
            second[c, row : row + ROWS, :] = 0.75 * start[c, row : row + ROWS, :] + 0.25 * (
                middle[c] + time_step * rates[c]
            )
    for row in range(top, top + cz, ROWS):
        middle, rates = block(second, row)
        for c in range(3):
            value = start[c, row : row + ROWS, :] * (1.0 / 3.0) + (2.0 / 3.0) * (
                middle[c] + time_step * rates[c]
            )
            out_ref[c, 0, row - top : row - top + ROWS, :] = value[:, 0:cx]


def advance(velocity, slab, shear, sizes):
    three, planes, cz, cx = velocity.shape
    zh, xh, corner = halos(velocity.reshape(three * planes, cz, cx), sizes)
    smem = pl.BlockSpec(memory_space=pltpu.SMEM)
    main = pl.BlockSpec((3, 1, cz, cx), lambda p: (0, p, 0, 0))

    def edge(sides, lanes):
        return pl.BlockSpec((sides, 3, 1, ROWS, lanes), lambda p: (0, 0, p, 0, 0))

    return pl.pallas_call(
        step_kernel,
        grid=(planes,),
        out_shape=jax.ShapeDtypeStruct(velocity.shape, f32),
        in_specs=[main, edge(2, cx), edge(2, cz), edge(4, LANES), smem, smem],
        out_specs=main,
        scratch_shapes=[pltpu.VMEM((3, cz + 4 * ROWS, cx + LANES), f32)] * 3,
        name="step",
    )(
        velocity,
        zh.reshape(2, three, planes, ROWS, cx),
        xh.reshape(2, three, planes, ROWS, cz),
        corner.reshape(4, three, planes, ROWS, LANES),
        slab,
        shear,
    )


def filter_kernel(
    sizes, planes, adv_ref, counts_ref, txh_hbm, txl_hbm, tzh_ref, tzl_ref, tth_ref, ttl_ref, gath,
    high, low, txh, txl, part_send, part_keep, part_recv, y_send, y_recv, z_send, z_recv, z_out,
    table_sem, ps_sem, pr_sem, ys_sem, yr_sem, zs_sem, zr_sem, os_sem, gr_sem, gy_sem, gp_sem,
):
    gx_n, gz_n, grp_n = sizes
    z_n = gz_n * grp_n
    y_n = gx_n // 2
    chunks, total_units, _, lanes = gath.shape
    units = total_units // gx_n
    _, cz, cx = adv_ref.shape
    gx = lax.axis_index("gx")
    z = lax.axis_index("gz") * grp_n + lax.axis_index("grp")
    y, core = lax.div(gx, 2), lax.rem(gx, 2)
    other = 1 - core

    def at_x(to_y, to_core):
        return {"gx": 2 * to_y + to_core, "gz": lax.axis_index("gz"), "grp": lax.axis_index("grp")}

    def at_z(to_z):
        to_z = jnp.int32(to_z)
        return {"gx": gx, "gz": lax.div(to_z, grp_n), "grp": lax.rem(to_z, grp_n)}

    def remote(src, dst, send, recv, device):
        return pltpu.make_async_remote_copy(
            src_ref=src, dst_ref=dst, send_sem=send, recv_sem=recv, device_id=device, device_id_type=MESH
        )

    barrier = pltpu.get_barrier_semaphore()
    friends = [at_x(y, other)]
    friends += [at_x(lax.rem(y + d, y_n), core) for d in range(1, y_n)]
    friends += [at_z(lax.rem(z + d, z_n)) for d in range(1, z_n)]
    for friend in friends:
        pl.semaphore_signal(barrier, inc=1, device_id=friend, device_id_type=MESH)

    mine = pl.ds(pl.multiple_of(gx * cx, cx), cx)
    tables = [
        pltpu.make_async_copy(txh_hbm.at[mine, :], txh, table_sem.at[0]),
        pltpu.make_async_copy(txl_hbm.at[mine, :], txl, table_sem.at[1]),
    ]
    for copy in tables:
        copy.start()

    def put(unit, values):
        h, l = split(values)
        high[unit] = h
        low[unit] = l

    def prepare(p, carry):
        parts = [adv_ref[i * planes + p] for i in range(3)]
        for i in range(3):
            put(p * FIELDS + i, parts[i])
        for q, (a, b) in enumerate(zip(pair_first, pair_second)):
            put(p * FIELDS + 3 + q, parts[a] * parts[b])
        return carry

    lax.fori_loop(0, planes, prepare, 0)
    for unit in range(planes * FIELDS, total_units):
        high[unit] = jnp.zeros((cz, cx), bf16)
        low[unit] = jnp.zeros((cz, cx), bf16)
    for copy in tables:
        copy.wait()

    def analyse(block, target, d):
        chosen = pl.ds(block * units, units)
        rows = (high[chosen].reshape(units * cz, cx), low[chosen].reshape(units * cz, cx))
        sums = dot3(rows, (txh[...], txl[...]))
        for h in range(chunks):
            target[h, d] = sums[:, h * lanes : (h + 1) * lanes].reshape(units, cz, lanes)

    def to_partner(h, d):
        return remote(
            part_send.at[h, d], part_recv.at[h, d], ps_sem.at[h, d], pr_sem.at[h, d], at_x(y, other)
        )

    def to_y(h, d):
        return remote(
            y_send.at[h, d - 1], y_recv.at[h, d - 1], ys_sem.at[h, d - 1], yr_sem.at[h, d - 1],
            at_x(lax.rem(y + d, y_n), core),
        )

    def send_y(h, d):
        to_partner(h, d).wait_recv()
        y_send[h, d - 1] = part_keep[h, d] + part_recv[h, d]
        to_y(h, d).start()

    def forward(h, k):
        return remote(z_send.at[h, k], z_recv.at[h, z], zs_sem.at[h, k], zr_sem.at[h, z], at_z(k))

    unit = gx * units + z

    def back(h, s, slot):
        return remote(z_out.at[h, s], gath.at[h, slot], os_sem.at[h, s], gr_sem.at[h, slot], at_z(s))

    def send_z(h):
        to_partner(h, 0).wait_recv()
        for d in range(1, y_n):
            to_y(h, d).wait_recv()
        for k in range(units):
            total = part_keep[h, 0, k] + part_recv[h, 0, k]
            for d in range(1, y_n):
                total = total + y_recv[h, d - 1, k]
            z_send[h, k] = total

            @pl.when(z != k)
            def _():
                forward(h, k).start()

            @pl.when(z == k)
            def _():
                z_recv[h, z] = total

    def filter_lines(h):
        for s in range(z_n):

            @pl.when(z != s)
            def _():
                remote(
                    z_send.at[h, 0], z_recv.at[h, s], zs_sem.at[h, 0], zr_sem.at[h, s], at_z(s)
                ).wait_recv()

        plane = jnp.minimum(lax.div(unit, FIELDS), planes - 1)
        limit_x, limit_z = counts_ref[plane, 0], counts_ref[plane, 1]

        def numbers(axis, start):
            column = lax.broadcasted_iota(jnp.int32, (MODES, lanes), axis) + start
            half = MODES // 2
            return jnp.where(column < half, column, column - half + 1), column

        def weights(column, length):
            return jnp.where(column == 0, f32(1.0 / length), f32(2.0 / length))

        kz, nz = numbers(0, 0)
        kx, nx = numbers(1, h * lanes)
        scale = weights(nz, z_n * cz) * weights(nx, gx_n * cx)
        scale = jnp.where((kz <= limit_z) & (kx <= limit_x), scale, 0.0)
        lines = split(z_recv[h].reshape(z_n * cz, lanes))
        spectral = dot3((tth_ref[...], ttl_ref[...]), lines) * scale
        z_out[h] = dot3((tzh_ref[...], tzl_ref[...]), split(spectral)).reshape(z_n, cz, lanes)
        for s in range(z_n):

            @pl.when(z != s)
            def _():
                back(h, s, unit).start()

            @pl.when(z == s)
            def _():
                gath[h, unit] = z_out[h, s]

    def spread(h, slot, k, d):
        return remote(
            gath.at[h, slot], gath.at[h, slot], gy_sem.at[h, d - 1, k], gr_sem.at[h, slot],
            at_x(lax.rem(y + d, y_n), core),
        )

    def share(h, slot, d, k):
        return remote(
            gath.at[h, slot], gath.at[h, slot], gp_sem.at[h, d, k], gr_sem.at[h, slot], at_x(y, other)
        )

    def spread_own(h):
        for k in range(units):
            slot = gx * units + k

            @pl.when(z != k)
            def _():
                back(h, 0, slot).wait_recv()

            for d in range(1, y_n):
                spread(h, slot, k, d).start()
            share(h, slot, 0, k).start()

    def share_others(h):
        for d in range(1, y_n):
            for k in range(units):
                slot = (2 * lax.rem(y + d, y_n) + core) * units + k
                back(h, 0, slot).wait_recv()
                share(h, slot, d, k).start()

    order = list(range(1, y_n)) + [0]
    first = True
    for d in order:
        analyse(2 * lax.rem(y + d, y_n) + other, part_send, d)
        if first:
            pl.semaphore_wait(barrier, len(friends))
            first = False
        for h in range(chunks):
            to_partner(h, d).start()
        analyse(2 * lax.rem(y + d, y_n) + core, part_keep, d)
        if d:
            for h in range(chunks):
                send_y(h, d)
    for h in range(chunks):
        send_z(h)

    @pl.when(z < units)
    def _():
        filter_lines(0)

    for h in range(chunks):
        spread_own(h)
        if h + 1 < chunks:

            @pl.when(z < units)
            def _():
                filter_lines(h + 1)

        share_others(h)
    for h in range(chunks):
        for d in range(y_n):
            for k in range(units):
                back(h, 0, (2 * lax.rem(y + d, y_n) + other) * units + k).wait_recv()

    for h in range(chunks):
        for d in range(y_n):
            to_partner(h, d).wait_send()
        for d in range(1, y_n):
            to_y(h, d).wait_send()
        for k in range(units):

            @pl.when(z != k)
            def _():
                forward(h, k).wait_send()

            for d in range(1, y_n):
                spread(h, gx * units + k, k, d).wait_send()
            for d in range(y_n):
                share(h, gx * units + k, d, k).wait_send()

        @pl.when(z < units)
        def _():
            for s in range(z_n):

                @pl.when(z != s)
                def _():
                    back(h, s, unit).wait_send()


def synthesis_kernel(gath_ref, txh_hbm, txl_hbm, out_ref, txh, txl, table_sem):
    chunks, _, cz, _ = gath_ref.shape
    cx = txh.shape[0]

    @pl.when(pl.program_id(0) == 0)
    def _():
        mine = pl.ds(pl.multiple_of(lax.axis_index("gx") * cx, cx), cx)
        copies = [
            pltpu.make_async_copy(txh_hbm.at[mine, :], txh, table_sem.at[0]),
            pltpu.make_async_copy(txl_hbm.at[mine, :], txl, table_sem.at[1]),
        ]
        for copy in copies:
            copy.start()
        for copy in copies:
            copy.wait()

    rows = jnp.concatenate([gath_ref[h].reshape(FIELDS * cz, -1) for h in range(chunks)], axis=1)
    filtered = dot3(split(rows), (txh[...], txl[...]), ((1,), (1,))).reshape(FIELDS, cz, cx)
    for q, (a, b) in enumerate(zip(pair_first, pair_second)):
        out_ref[q, 0] = filtered[3 + q] - filtered[a] * filtered[b]


def filtered_stress(advanced, mode_counts, sizes):
    gx_n, gz_n, grp_n = sizes
    z_n = gz_n * grp_n
    y_n = gx_n // 2
    count, cz, cx = advanced.shape
    planes = count // 3
    units = -(-FIELDS * planes // gx_n)
    assert gx_n % 2 == 0 and units <= z_n
    txh, txl = (jnp.asarray(t) for t in split_table(wave_table(cx * gx_n)))
    table_z = wave_table(cz * z_n)
    tzh, tzl = split_table(table_z)
    tth, ttl = split_table(table_z.T)
    dma = pltpu.SemaphoreType.DMA
    vmem = pl.BlockSpec(memory_space=pltpu.VMEM)
    anywhere = pl.BlockSpec(memory_space=pl.ANY)
    others = max(y_n - 1, 1)
    total = gx_n * units
    chunks = 2
    lanes = MODES // chunks
    gathered = pl.pallas_call(
        functools.partial(filter_kernel, sizes, planes),
        out_shape=jax.ShapeDtypeStruct((chunks, total, cz, lanes), f32),
        in_specs=[vmem, pl.BlockSpec(memory_space=pltpu.SMEM), anywhere, anywhere, vmem, vmem, vmem, vmem],
        out_specs=vmem,
        scratch_shapes=[
            pltpu.VMEM((total, cz, cx), bf16),
            pltpu.VMEM((total, cz, cx), bf16),
            pltpu.VMEM((cx, MODES), bf16),
            pltpu.VMEM((cx, MODES), bf16),
            pltpu.VMEM((chunks, y_n, units, cz, lanes), f32),
            pltpu.VMEM((chunks, y_n, units, cz, lanes), f32),
            pltpu.VMEM((chunks, y_n, units, cz, lanes), f32),
            pltpu.VMEM((chunks, others, units, cz, lanes), f32),
            pltpu.VMEM((chunks, others, units, cz, lanes), f32),
            pltpu.VMEM((chunks, units, cz, lanes), f32),
            pltpu.VMEM((chunks, z_n, cz, lanes), f32),
            pltpu.VMEM((chunks, z_n, cz, lanes), f32),
            dma((2,)),
            dma((chunks, y_n)),
            dma((chunks, y_n)),
            dma((chunks, others)),
            dma((chunks, others)),
            dma((chunks, units)),
            dma((chunks, z_n)),
            dma((chunks, z_n)),
            dma((chunks, total)),
            dma((chunks, others, units)),
            dma((chunks, y_n, units)),
        ],
        compiler_params=pltpu.CompilerParams(collective_id=1, has_side_effects=True),
        name="filter",
    )(advanced, mode_counts, txh, txl, *(jnp.asarray(t) for t in (tzh, tzl, tth, ttl)))
    return pl.pallas_call(
        synthesis_kernel,
        grid=(planes,),
        out_shape=jax.ShapeDtypeStruct((6, planes, cz, cx), f32),
        in_specs=[
            pl.BlockSpec((chunks, FIELDS, cz, lanes), lambda p: (0, p, 0, 0)), anywhere, anywhere
        ],
        out_specs=pl.BlockSpec((6, 1, cz, cx), lambda p: (0, p, 0, 0)),
        scratch_shapes=[pltpu.VMEM((cx, MODES), bf16), pltpu.VMEM((cx, MODES), bf16), dma((2,))],
        name="synthesis",
    )(gathered, txh, txl)


def local(sizes, velocity, slab, shear, mode_counts):
    three, planes, cz, cx = velocity.shape
    advanced = advance(velocity, slab, shear, sizes)
    stress = filtered_stress(advanced.reshape(three * planes, cz, cx), mode_counts, sizes)
    return advanced, stress


def solution(mesh):
    sizes = (mesh.shape["gx"], mesh.shape["gz"], mesh.shape["grp"])
    spread = P(None, None, ("gz", "grp"), "gx")
    return jax.shard_map(
        functools.partial(local, sizes),
        mesh=mesh,
        in_specs=(spread, P(), P(), P()),
        out_specs=(spread, spread),
        check_vma=False,
    )
```

```python
import functools
import math

import jax
import jax.numpy as jnp
import numpy as np
from jax import lax
from jax.experimental import pallas as pl
from jax.experimental.pallas import tpu as pltpu
from jax.sharding import PartitionSpec as P

MODES = 256
FIELDS = 9
MESH = pl.DeviceIdType.MESH
ROWS = 8
LANES = 128

molecular_diffusivity = 0.4
time_step = 0.2
pair_first = (0, 0, 0, 1, 1, 2)
pair_second = (0, 1, 2, 1, 2, 2)
f32 = jnp.float32
bf16 = jnp.bfloat16


def wave_table(length):
    column = np.arange(MODES)
    half = MODES // 2
    numbers = np.where(column < half, column, column - half + 1)
    angles = (np.arange(length)[:, None] * numbers[None, :] % length) * (2.0 * math.pi / length)
    return np.where(column[None, :] < half, np.cos(angles), np.sin(angles)).astype(np.float32)


def split_table(table):
    high = table.astype(bf16)
    low = (table - high.astype(np.float32)).astype(bf16)
    return high, low


def split(values):
    high = values.astype(bf16)
    return high, (values - high.astype(f32)).astype(bf16)


def dot3(a, b, contract=((1,), (0,))):
    def one(x, y):
        return lax.dot_general(x, y, (contract, ((), ())), preferred_element_type=f32)

    return one(a[0], b[0]) + (one(a[0], b[1]) + one(a[1], b[0]))


def halo_kernel(sizes, v_ref, zh_ref, xh_ref, corner_ref, strips, send_sem, recv_sem):
    gx_n, gz_n, grp_n = sizes
    z_n = gz_n * grp_n
    count, cz, cx = v_ref.shape
    gx = lax.axis_index("gx")
    z = lax.axis_index("gz") * grp_n + lax.axis_index("grp")
    steps = [(dx, dz) for dx in (-1, 0, 1) for dz in (-1, 0, 1) if dx or dz]

    def device(dx, dz):
        to_z = lax.rem(z + dz + z_n, z_n)
        return {
            "gx": lax.rem(gx + dx + gx_n, gx_n),
            "gz": lax.div(to_z, grp_n),
            "grp": lax.rem(to_z, grp_n),
        }

    barrier = pltpu.get_barrier_semaphore()
    for dx, dz in steps:
        pl.semaphore_signal(barrier, inc=1, device_id=device(dx, dz), device_id_type=MESH)
    for c in range(count):
        strips[0, c] = v_ref[c, :, 0:LANES].T[0:ROWS]
        strips[1, c] = v_ref[c, :, cx - LANES : cx].T[LANES - ROWS : LANES]
    pl.semaphore_wait(barrier, len(steps))
    edge_x = {1: pl.ds(cx - LANES, LANES), -1: pl.ds(0, LANES), 0: pl.ds(0, cx)}
    edge_z = {1: pl.ds(cz - ROWS, ROWS), -1: pl.ds(0, ROWS)}
    copies = []
    for index, (dx, dz) in enumerate(steps):
        side_x, side_z = int(dx > 0), int(dz > 0)
        if dz == 0:
            source, target = strips.at[side_x], xh_ref.at[side_x]
        else:
            source = v_ref.at[:, edge_z[dz], edge_x[dx]]
            target = zh_ref.at[side_z] if dx == 0 else corner_ref.at[2 * side_z + side_x]
        copies.append(
            pltpu.make_async_remote_copy(
                src_ref=source,
                dst_ref=target,
                send_sem=send_sem.at[index],
                recv_sem=recv_sem.at[index],
                device_id=device(dx, dz),
                device_id_type=MESH,
            )
        )
    for copy in copies:
        copy.start()
    for copy in copies:
        copy.wait()


def halos(velocity, sizes):
    count, cz, cx = velocity.shape
    vmem = pl.BlockSpec(memory_space=pltpu.VMEM)
    return pl.pallas_call(
        functools.partial(halo_kernel, sizes),
        out_shape=(
            jax.ShapeDtypeStruct((2, count, ROWS, cx), f32),
            jax.ShapeDtypeStruct((2, count, ROWS, cz), f32),
            jax.ShapeDtypeStruct((4, count, ROWS, LANES), f32),
        ),
        in_specs=[vmem],
        out_specs=(vmem, vmem, vmem),
        scratch_shapes=[
            pltpu.VMEM((2, count, ROWS, cz), f32),
            pltpu.SemaphoreType.DMA((8,)),
            pltpu.SemaphoreType.DMA((8,)),
        ],
        compiler_params=pltpu.CompilerParams(collective_id=0, has_side_effects=True),
        name="halo",
    )(velocity)


def step_kernel(v_ref, zh_ref, xh_ref, corner_ref, slab_ref, shear_ref, out_ref, start, first, second):
    p = pl.program_id(0)
    slab, shear = slab_ref[p], shear_ref[p]
    _, _, cz, cx = v_ref.shape
    top = 2 * ROWS
    lane = lax.broadcasted_iota(jnp.int32, (ROWS, LANES), 1)
    width = cx + LANES
    for c in range(3):
        start[c, top : top + cz, 0:cx] = v_ref[c, 0]
        strip = jnp.concatenate(
            [xh_ref[0, c, 0], jnp.zeros((LANES - 2 * ROWS, cz), f32), xh_ref[1, c, 0]], axis=0
        )
        start[c, top : top + cz, cx:width] = strip.T
        for side, row in ((1, top - ROWS), (0, top + cz)):
            start[c, row : row + ROWS, 0:cx] = zh_ref[side, c, 0]
            start[c, row : row + ROWS, cx:width] = jnp.where(
                lane < LANES // 2, corner_ref[2 * side, c, 0], corner_ref[2 * side + 1, c, 0]
            )

    def block(source, row):
        middle = [source[c, row : row + ROWS, :] for c in range(3)]
        rates = []
        for c in range(3):
            north = source[c, row + 1 : row + 1 + ROWS, :]
            south = source[c, row - 1 : row - 1 + ROWS, :]
            east = pltpu.roll(middle[c], width - 1, 1)
            west = pltpu.roll(middle[c], 1, 1)
            value = (
                -(slab + middle[0]) * ((east - west) * 0.5)
                - middle[2] * ((north - south) * 0.5)
                + molecular_diffusivity * (east + west + north + south - 4.0 * middle[c])
            )
            rates.append(value - shear * middle[1] if c == 0 else value)
        return middle, rates

    for row in range(ROWS, top + cz + ROWS, ROWS):
        middle, rates = block(start, row)
        for c in range(3):
            first[c, row : row + ROWS, :] = middle[c] + time_step * rates[c]
    for row in range(ROWS, top + cz + ROWS, ROWS):
        middle, rates = block(first, row)
        for c in range(3):
            second[c, row : row + ROWS, :] = 0.75 * start[c, row : row + ROWS, :] + 0.25 * (
                middle[c] + time_step * rates[c]
            )
    for row in range(top, top + cz, ROWS):
        middle, rates = block(second, row)
        for c in range(3):
            value = start[c, row : row + ROWS, :] * (1.0 / 3.0) + (2.0 / 3.0) * (
                middle[c] + time_step * rates[c]
            )
            out_ref[c, 0, row - top : row - top + ROWS, :] = value[:, 0:cx]


def advance(velocity, slab, shear, sizes):
    three, planes, cz, cx = velocity.shape
    zh, xh, corner = halos(velocity.reshape(three * planes, cz, cx), sizes)
    smem = pl.BlockSpec(memory_space=pltpu.SMEM)
    main = pl.BlockSpec((3, 1, cz, cx), lambda p: (0, p, 0, 0))

    def edge(sides, lanes):
        return pl.BlockSpec((sides, 3, 1, ROWS, lanes), lambda p: (0, 0, p, 0, 0))

    return pl.pallas_call(
        step_kernel,
        grid=(planes,),
        out_shape=jax.ShapeDtypeStruct(velocity.shape, f32),
        in_specs=[main, edge(2, cx), edge(2, cz), edge(4, LANES), smem, smem],
        out_specs=main,
        scratch_shapes=[pltpu.VMEM((3, cz + 4 * ROWS, cx + LANES), f32)] * 3,
        name="step",
    )(
        velocity,
        zh.reshape(2, three, planes, ROWS, cx),
        xh.reshape(2, three, planes, ROWS, cz),
        corner.reshape(4, three, planes, ROWS, LANES),
        slab,
        shear,
    )


def filter_kernel(
    sizes, planes, adv_ref, counts_ref, txh_hbm, txl_hbm, tzh_ref, tzl_ref, tth_ref, ttl_ref, gath,
    high, low, txh, txl, part_send, part_keep, part_recv, y_send, y_recv, z_send, z_recv, z_out,
    table_sem, ps_sem, pr_sem, ys_sem, yr_sem, zs_sem, zr_sem, os_sem, gr_sem, gy_sem, gp_sem,
):
    gx_n, gz_n, grp_n = sizes
    z_n = gz_n * grp_n
    y_n = gx_n // 2
    chunks, total_units, _, lanes = gath.shape
    units = total_units // gx_n
    _, cz, cx = adv_ref.shape
    gx = lax.axis_index("gx")
    z = lax.axis_index("gz") * grp_n + lax.axis_index("grp")
    y, core = lax.div(gx, 2), lax.rem(gx, 2)
    other = 1 - core

    def at_x(to_y, to_core):
        return {"gx": 2 * to_y + to_core, "gz": lax.axis_index("gz"), "grp": lax.axis_index("grp")}

    def at_z(to_z):
        to_z = jnp.int32(to_z)
        return {"gx": gx, "gz": lax.div(to_z, grp_n), "grp": lax.rem(to_z, grp_n)}

    def remote(src, dst, send, recv, device):
        return pltpu.make_async_remote_copy(
            src_ref=src, dst_ref=dst, send_sem=send, recv_sem=recv, device_id=device, device_id_type=MESH
        )

    barrier = pltpu.get_barrier_semaphore()
    friends = [at_x(y, other)]
    friends += [at_x(lax.rem(y + d, y_n), core) for d in range(1, y_n)]
    friends += [at_z(lax.rem(z + d, z_n)) for d in range(1, z_n)]
    for friend in friends:
        pl.semaphore_signal(barrier, inc=1, device_id=friend, device_id_type=MESH)

    mine = pl.ds(pl.multiple_of(gx * cx, cx), cx)
    tables = [
        pltpu.make_async_copy(txh_hbm.at[mine, :], txh, table_sem.at[0]),
        pltpu.make_async_copy(txl_hbm.at[mine, :], txl, table_sem.at[1]),
    ]
    for copy in tables:
        copy.start()

    def put(unit, values):
        h, l = split(values)
        high[unit] = h
        low[unit] = l

    def prepare(p, carry):
        parts = [adv_ref[i * planes + p] for i in range(3)]
        for i in range(3):
            put(p * FIELDS + i, parts[i])
        for q, (a, b) in enumerate(zip(pair_first, pair_second)):
            put(p * FIELDS + 3 + q, parts[a] * parts[b])
        return carry

    lax.fori_loop(0, planes, prepare, 0)
    for unit in range(planes * FIELDS, total_units):
        high[unit] = jnp.zeros((cz, cx), bf16)
        low[unit] = jnp.zeros((cz, cx), bf16)
    for copy in tables:
        copy.wait()

    def analyse(block, target, d):
        chosen = pl.ds(block * units, units)
        rows = (high[chosen].reshape(units * cz, cx), low[chosen].reshape(units * cz, cx))
        sums = dot3(rows, (txh[...], txl[...]))
        for h in range(chunks):
            target[h, d] = sums[:, h * lanes : (h + 1) * lanes].reshape(units, cz, lanes)

    def to_partner(h, d):
        return remote(
            part_send.at[h, d], part_recv.at[h, d], ps_sem.at[h, d], pr_sem.at[h, d], at_x(y, other)
        )

    def to_y(h, d, k):
        return remote(
            y_send.at[h, d - 1, k], y_recv.at[h, d - 1, k], ys_sem.at[h, d - 1, k], yr_sem.at[h, d - 1, k],
            at_x(lax.rem(y + d, y_n), core),
        )

    turns = [lax.rem(z + i, units) for i in range(units)]

    def send_y(h, d):
        to_partner(h, d).wait_recv()
        for k in turns:
            y_send[h, d - 1, k] = part_keep[h, d, k] + part_recv[h, d, k]
            to_y(h, d, k).start()

    def forward(h, k):
        return remote(z_send.at[h, k], z_recv.at[h, z], zs_sem.at[h, k], zr_sem.at[h, z], at_z(k))

    unit = gx * units + z

    def back(h, s, slot):
        return remote(z_out.at[h, s], gath.at[h, slot], os_sem.at[h, s], gr_sem.at[h, slot], at_z(s))

    def send_z(h):
        to_partner(h, 0).wait_recv()
        for k in turns:
            for d in range(1, y_n):
                to_y(h, d, k).wait_recv()
            total = part_keep[h, 0, k] + part_recv[h, 0, k]
            for d in range(1, y_n):
                total = total + y_recv[h, d - 1, k]
            z_send[h, k] = total

            @pl.when(z != k)
            def _():
                forward(h, k).start()

            @pl.when(z == k)
            def _():
                z_recv[h, z] = total

    def filter_lines(h):
        for s in range(z_n):

            @pl.when(z != s)
            def _():
                remote(
                    z_send.at[h, 0], z_recv.at[h, s], zs_sem.at[h, 0], zr_sem.at[h, s], at_z(s)
                ).wait_recv()

        plane = jnp.minimum(lax.div(unit, FIELDS), planes - 1)
        limit_x, limit_z = counts_ref[plane, 0], counts_ref[plane, 1]

        def numbers(axis, start):
            column = lax.broadcasted_iota(jnp.int32, (MODES, lanes), axis) + start
            half = MODES // 2
            return jnp.where(column < half, column, column - half + 1), column

        def weights(column, length):
            return jnp.where(column == 0, f32(1.0 / length), f32(2.0 / length))

        kz, nz = numbers(0, 0)
        kx, nx = numbers(1, h * lanes)
        scale = weights(nz, z_n * cz) * weights(nx, gx_n * cx)
        scale = jnp.where((kz <= limit_z) & (kx <= limit_x), scale, 0.0)
        lines = split(z_recv[h].reshape(z_n * cz, lanes))
        spectral = dot3((tth_ref[...], ttl_ref[...]), lines) * scale
        z_out[h] = dot3((tzh_ref[...], tzl_ref[...]), split(spectral)).reshape(z_n, cz, lanes)
        for s in range(z_n):

            @pl.when(z != s)
            def _():
                back(h, s, unit).start()

            @pl.when(z == s)
            def _():
                gath[h, unit] = z_out[h, s]

    def spread(h, slot, k, d):
        return remote(
            gath.at[h, slot], gath.at[h, slot], gy_sem.at[h, d - 1, k], gr_sem.at[h, slot],
            at_x(lax.rem(y + d, y_n), core),
        )

    def share(h, slot, d, k):
        return remote(
            gath.at[h, slot], gath.at[h, slot], gp_sem.at[h, d, k], gr_sem.at[h, slot], at_x(y, other)
        )

    def spread_own(h):
        for k in range(units):
            slot = gx * units + k

            @pl.when(z != k)
            def _():
                back(h, 0, slot).wait_recv()

            for d in range(1, y_n):
                spread(h, slot, k, d).start()
            share(h, slot, 0, k).start()

    def share_others(h):
        for d in range(1, y_n):
            for k in range(units):
                slot = (2 * lax.rem(y + d, y_n) + core) * units + k
                back(h, 0, slot).wait_recv()
                share(h, slot, d, k).start()

    order = list(range(1, y_n)) + [0]
    first = True
    for d in order:
        analyse(2 * lax.rem(y + d, y_n) + other, part_send, d)
        if first:
            pl.semaphore_wait(barrier, len(friends))
            first = False
        for h in range(chunks):
            to_partner(h, d).start()
        analyse(2 * lax.rem(y + d, y_n) + core, part_keep, d)
        if d:
            for h in range(chunks):
                send_y(h, d)
    send_z(0)

    @pl.when(z < units)
    def _():
        filter_lines(0)

    for h in range(1, chunks):
        send_z(h)
    for h in range(chunks):
        spread_own(h)
        if h + 1 < chunks:

            @pl.when(z < units)
            def _():
                filter_lines(h + 1)

        share_others(h)
    for h in range(chunks):
        for d in range(y_n):
            for k in range(units):
                back(h, 0, (2 * lax.rem(y + d, y_n) + other) * units + k).wait_recv()

    for h in range(chunks):
        for d in range(y_n):
            to_partner(h, d).wait_send()
        for d in range(1, y_n):
            for k in range(units):
                to_y(h, d, k).wait_send()
        for k in range(units):

            @pl.when(z != k)
            def _():
                forward(h, k).wait_send()

            for d in range(1, y_n):
                spread(h, gx * units + k, k, d).wait_send()
            for d in range(y_n):
                share(h, gx * units + k, d, k).wait_send()

        @pl.when(z < units)
        def _():
            for s in range(z_n):

                @pl.when(z != s)
                def _():
                    back(h, s, unit).wait_send()


def synthesis_kernel(gath_ref, txh_hbm, txl_hbm, out_ref, txh, txl, table_sem):
    chunks, _, cz, _ = gath_ref.shape
    cx = txh.shape[0]

    @pl.when(pl.program_id(0) == 0)
    def _():
        mine = pl.ds(pl.multiple_of(lax.axis_index("gx") * cx, cx), cx)
        copies = [
            pltpu.make_async_copy(txh_hbm.at[mine, :], txh, table_sem.at[0]),
            pltpu.make_async_copy(txl_hbm.at[mine, :], txl, table_sem.at[1]),
        ]
        for copy in copies:
            copy.start()
        for copy in copies:
            copy.wait()

    rows = jnp.concatenate([gath_ref[h].reshape(FIELDS * cz, -1) for h in range(chunks)], axis=1)
    filtered = dot3(split(rows), (txh[...], txl[...]), ((1,), (1,))).reshape(FIELDS, cz, cx)
    for q, (a, b) in enumerate(zip(pair_first, pair_second)):
        out_ref[q, 0] = filtered[3 + q] - filtered[a] * filtered[b]


def filtered_stress(advanced, mode_counts, sizes):
    gx_n, gz_n, grp_n = sizes
    z_n = gz_n * grp_n
    y_n = gx_n // 2
    count, cz, cx = advanced.shape
    planes = count // 3
    units = -(-FIELDS * planes // gx_n)
    assert gx_n % 2 == 0 and units <= z_n
    txh, txl = (jnp.asarray(t) for t in split_table(wave_table(cx * gx_n)))
    table_z = wave_table(cz * z_n)
    tzh, tzl = split_table(table_z)
    tth, ttl = split_table(table_z.T)
    dma = pltpu.SemaphoreType.DMA
    vmem = pl.BlockSpec(memory_space=pltpu.VMEM)
    anywhere = pl.BlockSpec(memory_space=pl.ANY)
    others = max(y_n - 1, 1)
    total = gx_n * units
    chunks = 2
    lanes = MODES // chunks
    gathered = pl.pallas_call(
        functools.partial(filter_kernel, sizes, planes),
        out_shape=jax.ShapeDtypeStruct((chunks, total, cz, lanes), f32),
        in_specs=[vmem, pl.BlockSpec(memory_space=pltpu.SMEM), anywhere, anywhere, vmem, vmem, vmem, vmem],
        out_specs=vmem,
        scratch_shapes=[
            pltpu.VMEM((total, cz, cx), bf16),
            pltpu.VMEM((total, cz, cx), bf16),
            pltpu.VMEM((cx, MODES), bf16),
            pltpu.VMEM((cx, MODES), bf16),
            pltpu.VMEM((chunks, y_n, units, cz, lanes), f32),
            pltpu.VMEM((chunks, y_n, units, cz, lanes), f32),
            pltpu.VMEM((chunks, y_n, units, cz, lanes), f32),
            pltpu.VMEM((chunks, others, units, cz, lanes), f32),
            pltpu.VMEM((chunks, others, units, cz, lanes), f32),
            pltpu.VMEM((chunks, units, cz, lanes), f32),
            pltpu.VMEM((chunks, z_n, cz, lanes), f32),
            pltpu.VMEM((chunks, z_n, cz, lanes), f32),
            dma((2,)),
            dma((chunks, y_n)),
            dma((chunks, y_n)),
            dma((chunks, others, units)),
            dma((chunks, others, units)),
            dma((chunks, units)),
            dma((chunks, z_n)),
            dma((chunks, z_n)),
            dma((chunks, total)),
            dma((chunks, others, units)),
            dma((chunks, y_n, units)),
        ],
        compiler_params=pltpu.CompilerParams(collective_id=1, has_side_effects=True),
        name="filter",
    )(advanced, mode_counts, txh, txl, *(jnp.asarray(t) for t in (tzh, tzl, tth, ttl)))
    return pl.pallas_call(
        synthesis_kernel,
        grid=(planes,),
        out_shape=jax.ShapeDtypeStruct((6, planes, cz, cx), f32),
        in_specs=[
            pl.BlockSpec((chunks, FIELDS, cz, lanes), lambda p: (0, p, 0, 0)), anywhere, anywhere
        ],
        out_specs=pl.BlockSpec((6, 1, cz, cx), lambda p: (0, p, 0, 0)),
        scratch_shapes=[pltpu.VMEM((cx, MODES), bf16), pltpu.VMEM((cx, MODES), bf16), dma((2,))],
        name="synthesis",
    )(gathered, txh, txl)


def local(sizes, velocity, slab, shear, mode_counts):
    three, planes, cz, cx = velocity.shape
    advanced = advance(velocity, slab, shear, sizes)
    stress = filtered_stress(advanced.reshape(three * planes, cz, cx), mode_counts, sizes)
    return advanced, stress


def solution(mesh):
    sizes = (mesh.shape["gx"], mesh.shape["gz"], mesh.shape["grp"])
    spread = P(None, None, ("gz", "grp"), "gx")
    return jax.shard_map(
        functools.partial(local, sizes),
        mesh=mesh,
        in_specs=(spread, P(), P(), P()),
        out_specs=(spread, spread),
        check_vma=False,
    )
```

```python
import functools
import math

import jax
import jax.numpy as jnp
import numpy as np
from jax import lax
from jax.experimental import pallas as pl
from jax.experimental.pallas import tpu as pltpu
from jax.sharding import PartitionSpec as P

MODES = 256
FIELDS = 9
MESH = pl.DeviceIdType.MESH
ROWS = 8
LANES = 128

molecular_diffusivity = 0.4
time_step = 0.2
pair_first = (0, 0, 0, 1, 1, 2)
pair_second = (0, 1, 2, 1, 2, 2)
f32 = jnp.float32
bf16 = jnp.bfloat16


def wave_table(length):
    column = np.arange(MODES)
    half = MODES // 2
    numbers = np.where(column < half, column, column - half + 1)
    angles = (np.arange(length)[:, None] * numbers[None, :] % length) * (2.0 * math.pi / length)
    return np.where(column[None, :] < half, np.cos(angles), np.sin(angles)).astype(np.float32)


def split_table(table):
    high = table.astype(bf16)
    low = (table - high.astype(np.float32)).astype(bf16)
    return high, low


def split(values):
    high = values.astype(bf16)
    return high, (values - high.astype(f32)).astype(bf16)


def dot3(a, b, contract=((1,), (0,))):
    def one(x, y):
        return lax.dot_general(x, y, (contract, ((), ())), preferred_element_type=f32)

    return one(a[0], b[0]) + (one(a[0], b[1]) + one(a[1], b[0]))


def step_plane(p, planes, v_ref, zh_ref, xh_ref, corner_ref, slab, shear, out_ref, start, first, second):
    _, cz, cx = v_ref.shape
    top = 2 * ROWS
    lane = lax.broadcasted_iota(jnp.int32, (ROWS, LANES), 1)
    width = cx + LANES
    for c in range(3):
        start[c, top : top + cz, 0:cx] = v_ref[c * planes + p]
        strip = jnp.concatenate(
            [
                xh_ref[0, c * planes + p],
                jnp.zeros((LANES - 2 * ROWS, cz), f32),
                xh_ref[1, c * planes + p],
            ], axis=0
        )
        start[c, top : top + cz, cx:width] = strip.T
        for side, row in ((1, top - ROWS), (0, top + cz)):
            start[c, row : row + ROWS, 0:cx] = zh_ref[side, c * planes + p]
            start[c, row : row + ROWS, cx:width] = jnp.where(
                lane < LANES // 2,
                corner_ref[2 * side, c * planes + p],
                corner_ref[2 * side + 1, c * planes + p],
            )

    def block(source, row):
        middle = [source[c, row : row + ROWS, :] for c in range(3)]
        rates = []
        for c in range(3):
            north = source[c, row + 1 : row + 1 + ROWS, :]
            south = source[c, row - 1 : row - 1 + ROWS, :]
            east = pltpu.roll(middle[c], width - 1, 1)
            west = pltpu.roll(middle[c], 1, 1)
            value = (
                -(slab + middle[0]) * ((east - west) * 0.5)
                - middle[2] * ((north - south) * 0.5)
                + molecular_diffusivity * (east + west + north + south - 4.0 * middle[c])
            )
            rates.append(value - shear * middle[1] if c == 0 else value)
        return middle, rates

    for row in range(ROWS, top + cz + ROWS, ROWS):
        middle, rates = block(start, row)
        for c in range(3):
            first[c, row : row + ROWS, :] = middle[c] + time_step * rates[c]
    for row in range(ROWS, top + cz + ROWS, ROWS):
        middle, rates = block(first, row)
        for c in range(3):
            second[c, row : row + ROWS, :] = 0.75 * start[c, row : row + ROWS, :] + 0.25 * (
                middle[c] + time_step * rates[c]
            )
    for row in range(top, top + cz, ROWS):
        middle, rates = block(second, row)
        for c in range(3):
            value = start[c, row : row + ROWS, :] * (1.0 / 3.0) + (2.0 / 3.0) * (
                middle[c] + time_step * rates[c]
            )
            out_ref[c * planes + p, row - top : row - top + ROWS, :] = value[:, 0:cx]


def filter_kernel(
    sizes, planes, v_ref, slab_ref, shear_ref, counts_ref, txh_hbm, txl_hbm, tzh_ref, tzl_ref, tth_ref,
    ttl_ref, gath, adv_ref, strips, zh_ref, xh_ref, corner_ref, start, first_ref, second_ref,
    high, low, txh, txl, part_send, part_keep, part_recv, y_send, y_recv, z_send, z_recv, z_out,
    table_sem, ps_sem, pr_sem, ys_sem, yr_sem, zs_sem, zr_sem, os_sem, gr_sem, gy_sem, gp_sem,
    hs_sem, hr_sem,
):
    gx_n, gz_n, grp_n = sizes
    z_n = gz_n * grp_n
    y_n = gx_n // 2
    chunks, total_units, _, lanes = gath.shape
    units = total_units // gx_n
    count, cz, cx = adv_ref.shape
    gx = lax.axis_index("gx")
    z = lax.axis_index("gz") * grp_n + lax.axis_index("grp")
    y, core = lax.div(gx, 2), lax.rem(gx, 2)
    other = 1 - core

    def at_x(to_y, to_core):
        return {"gx": 2 * to_y + to_core, "gz": lax.axis_index("gz"), "grp": lax.axis_index("grp")}

    def at_z(to_z):
        to_z = jnp.int32(to_z)
        return {"gx": gx, "gz": lax.div(to_z, grp_n), "grp": lax.rem(to_z, grp_n)}

    def remote(src, dst, send, recv, device):
        return pltpu.make_async_remote_copy(
            src_ref=src, dst_ref=dst, send_sem=send, recv_sem=recv, device_id=device, device_id_type=MESH
        )

    barrier = pltpu.get_barrier_semaphore()
    friends = [at_x(y, other)]
    friends += [at_x(lax.rem(y + d, y_n), core) for d in range(1, y_n)]
    friends += [at_z(lax.rem(z + d, z_n)) for d in range(1, z_n)]
    steps = [(dx, dz) for dx in (-1, 0, 1) for dz in (-1, 0, 1) if dx or dz]

    def near(dx, dz):
        to_z = lax.rem(z + dz + z_n, z_n)
        return {
            "gx": lax.rem(gx + dx + gx_n, gx_n),
            "gz": lax.div(to_z, grp_n),
            "grp": lax.rem(to_z, grp_n),
        }

    friends += [near(dx, dz) for dx, dz in steps]
    for friend in friends:
        pl.semaphore_signal(barrier, inc=1, device_id=friend, device_id_type=MESH)

    mine = pl.ds(pl.multiple_of(gx * cx, cx), cx)
    tables = [
        pltpu.make_async_copy(txh_hbm.at[mine, :], txh, table_sem.at[0]),
        pltpu.make_async_copy(txl_hbm.at[mine, :], txl, table_sem.at[1]),
    ]
    for copy in tables:
        copy.start()

    for c in range(count):
        strips[0, c] = v_ref[c, :, 0:LANES].T[0:ROWS]
        strips[1, c] = v_ref[c, :, cx - LANES : cx].T[LANES - ROWS : LANES]
    pl.semaphore_wait(barrier, len(friends))
    edge_x = {1: pl.ds(cx - LANES, LANES), -1: pl.ds(0, LANES), 0: pl.ds(0, cx)}
    edge_z = {1: pl.ds(cz - ROWS, ROWS), -1: pl.ds(0, ROWS)}
    edges = []
    for index, (dx, dz) in enumerate(steps):
        side_x, side_z = int(dx > 0), int(dz > 0)
        if dz == 0:
            source, target = strips.at[side_x], xh_ref.at[side_x]
        else:
            source = v_ref.at[:, edge_z[dz], edge_x[dx]]
            target = zh_ref.at[side_z] if dx == 0 else corner_ref.at[2 * side_z + side_x]
        edges.append(remote(source, target, hs_sem.at[index], hr_sem.at[index], near(dx, dz)))
    for copy in edges:
        copy.start()
    for copy in edges:
        copy.wait()

    def put(unit, values):
        h, l = split(values)
        high[unit] = h
        low[unit] = l

    def prepare(p, carry):
        step_plane(
            p, planes, v_ref, zh_ref, xh_ref, corner_ref, slab_ref[p], shear_ref[p], adv_ref, start,
            first_ref, second_ref,
        )
        parts = [adv_ref[i * planes + p] for i in range(3)]
        for i in range(3):
            put(p * FIELDS + i, parts[i])
        for q, (a, b) in enumerate(zip(pair_first, pair_second)):
            put(p * FIELDS + 3 + q, parts[a] * parts[b])
        return carry

    lax.fori_loop(0, planes, prepare, 0)
    for unit in range(planes * FIELDS, total_units):
        high[unit] = jnp.zeros((cz, cx), bf16)
        low[unit] = jnp.zeros((cz, cx), bf16)
    for copy in tables:
        copy.wait()

    def analyse(block, target, d):
        chosen = pl.ds(block * units, units)
        rows = (high[chosen].reshape(units * cz, cx), low[chosen].reshape(units * cz, cx))
        sums = dot3(rows, (txh[...], txl[...]))
        for h in range(chunks):
            target[h, d] = sums[:, h * lanes : (h + 1) * lanes].reshape(units, cz, lanes)

    def to_partner(h, d):
        return remote(
            part_send.at[h, d], part_recv.at[h, d], ps_sem.at[h, d], pr_sem.at[h, d], at_x(y, other)
        )

    def to_y(h, d, k):
        return remote(
            y_send.at[h, d - 1, k], y_recv.at[h, d - 1, k], ys_sem.at[h, d - 1, k], yr_sem.at[h, d - 1, k],
            at_x(lax.rem(y + d, y_n), core),
        )

    turns = [lax.rem(z + i, units) for i in range(units)]

    def send_y(h, d):
        to_partner(h, d).wait_recv()
        for k in turns:
            y_send[h, d - 1, k] = part_keep[h, d, k] + part_recv[h, d, k]
            to_y(h, d, k).start()

    def forward(h, k):
        return remote(z_send.at[h, k], z_recv.at[h, z], zs_sem.at[h, k], zr_sem.at[h, z], at_z(k))

    unit = gx * units + z

    def back(h, s, slot):
        return remote(z_out.at[h, s], gath.at[h, slot], os_sem.at[h, s], gr_sem.at[h, slot], at_z(s))

    def send_z(h):
        to_partner(h, 0).wait_recv()
        for k in turns:
            for d in range(1, y_n):
                to_y(h, d, k).wait_recv()
            total = part_keep[h, 0, k] + part_recv[h, 0, k]
            for d in range(1, y_n):
                total = total + y_recv[h, d - 1, k]
            z_send[h, k] = total

            @pl.when(z != k)
            def _():
                forward(h, k).start()

            @pl.when(z == k)
            def _():
                z_recv[h, z] = total

    def filter_lines(h):
        for s in range(z_n):

            @pl.when(z != s)
            def _():
                remote(
                    z_send.at[h, 0], z_recv.at[h, s], zs_sem.at[h, 0], zr_sem.at[h, s], at_z(s)
                ).wait_recv()

        plane = jnp.minimum(lax.div(unit, FIELDS), planes - 1)
        limit_x, limit_z = counts_ref[plane, 0], counts_ref[plane, 1]

        def numbers(axis, start):
            column = lax.broadcasted_iota(jnp.int32, (MODES, lanes), axis) + start
            half = MODES // 2
            return jnp.where(column < half, column, column - half + 1), column

        def weights(column, length):
            return jnp.where(column == 0, f32(1.0 / length), f32(2.0 / length))

        kz, nz = numbers(0, 0)
        kx, nx = numbers(1, h * lanes)
        scale = weights(nz, z_n * cz) * weights(nx, gx_n * cx)
        scale = jnp.where((kz <= limit_z) & (kx <= limit_x), scale, 0.0)
        lines = split(z_recv[h].reshape(z_n * cz, lanes))
        spectral = dot3((tth_ref[...], ttl_ref[...]), lines) * scale
        z_out[h] = dot3((tzh_ref[...], tzl_ref[...]), split(spectral)).reshape(z_n, cz, lanes)
        for s in range(z_n):

            @pl.when(z != s)
            def _():
                back(h, s, unit).start()

            @pl.when(z == s)
            def _():
                gath[h, unit] = z_out[h, s]

    def spread(h, slot, k, d):
        return remote(
            gath.at[h, slot], gath.at[h, slot], gy_sem.at[h, d - 1, k], gr_sem.at[h, slot],
            at_x(lax.rem(y + d, y_n), core),
        )

    def share(h, slot, d, k):
        return remote(
            gath.at[h, slot], gath.at[h, slot], gp_sem.at[h, d, k], gr_sem.at[h, slot], at_x(y, other)
        )

    def spread_own(h):
        for k in range(units):
            slot = gx * units + k

            @pl.when(z != k)
            def _():
                back(h, 0, slot).wait_recv()

            for d in range(1, y_n):
                spread(h, slot, k, d).start()
            share(h, slot, 0, k).start()

    def share_others(h):
        for d in range(1, y_n):
            for k in range(units):
                slot = (2 * lax.rem(y + d, y_n) + core) * units + k
                back(h, 0, slot).wait_recv()
                share(h, slot, d, k).start()

    order = list(range(1, y_n)) + [0]
    for d in order:
        analyse(2 * lax.rem(y + d, y_n) + other, part_send, d)
        for h in range(chunks):
            to_partner(h, d).start()
        analyse(2 * lax.rem(y + d, y_n) + core, part_keep, d)
        if d:
            for h in range(chunks):
                send_y(h, d)
    send_z(0)

    @pl.when(z < units)
    def _():
        filter_lines(0)

    for h in range(1, chunks):
        send_z(h)
    for h in range(chunks):
        spread_own(h)
        if h + 1 < chunks:

            @pl.when(z < units)
            def _():
                filter_lines(h + 1)

        share_others(h)
    for h in range(chunks):
        for d in range(y_n):
            for k in range(units):
                back(h, 0, (2 * lax.rem(y + d, y_n) + other) * units + k).wait_recv()

    for h in range(chunks):
        for d in range(y_n):
            to_partner(h, d).wait_send()
        for d in range(1, y_n):
            for k in range(units):
                to_y(h, d, k).wait_send()
        for k in range(units):

            @pl.when(z != k)
            def _():
                forward(h, k).wait_send()

            for d in range(1, y_n):
                spread(h, gx * units + k, k, d).wait_send()
            for d in range(y_n):
                share(h, gx * units + k, d, k).wait_send()

        @pl.when(z < units)
        def _():
            for s in range(z_n):

                @pl.when(z != s)
                def _():
                    back(h, s, unit).wait_send()


def synthesis_kernel(gath_ref, txh_hbm, txl_hbm, out_ref, txh, txl, table_sem):
    chunks, _, cz, _ = gath_ref.shape
    cx = txh.shape[0]

    @pl.when(pl.program_id(0) == 0)
    def _():
        mine = pl.ds(pl.multiple_of(lax.axis_index("gx") * cx, cx), cx)
        copies = [
            pltpu.make_async_copy(txh_hbm.at[mine, :], txh, table_sem.at[0]),
            pltpu.make_async_copy(txl_hbm.at[mine, :], txl, table_sem.at[1]),
        ]
        for copy in copies:
            copy.start()
        for copy in copies:
            copy.wait()

    rows = jnp.concatenate([gath_ref[h].reshape(FIELDS * cz, -1) for h in range(chunks)], axis=1)
    filtered = dot3(split(rows), (txh[...], txl[...]), ((1,), (1,))).reshape(FIELDS, cz, cx)
    for q, (a, b) in enumerate(zip(pair_first, pair_second)):
        out_ref[q, 0] = filtered[3 + q] - filtered[a] * filtered[b]


def filtered_stress(velocity, slab, shear, mode_counts, sizes):
    gx_n, gz_n, grp_n = sizes
    z_n = gz_n * grp_n
    y_n = gx_n // 2
    three, planes, cz, cx = velocity.shape
    count = three * planes
    units = -(-FIELDS * planes // gx_n)
    assert gx_n % 2 == 0 and units <= z_n
    txh, txl = (jnp.asarray(t) for t in split_table(wave_table(cx * gx_n)))
    table_z = wave_table(cz * z_n)
    tzh, tzl = split_table(table_z)
    tth, ttl = split_table(table_z.T)
    dma = pltpu.SemaphoreType.DMA
    vmem = pl.BlockSpec(memory_space=pltpu.VMEM)
    anywhere = pl.BlockSpec(memory_space=pl.ANY)
    others = max(y_n - 1, 1)
    total = gx_n * units
    chunks = 2
    lanes = MODES // chunks
    smem = pl.BlockSpec(memory_space=pltpu.SMEM)
    gathered, advanced = pl.pallas_call(
        functools.partial(filter_kernel, sizes, planes),
        out_shape=(
            jax.ShapeDtypeStruct((chunks, total, cz, lanes), f32),
            jax.ShapeDtypeStruct((count, cz, cx), f32),
        ),
        in_specs=[vmem, smem, smem, smem, anywhere, anywhere, vmem, vmem, vmem, vmem],
        out_specs=(vmem, vmem),
        scratch_shapes=[
            pltpu.VMEM((2, count, ROWS, cz), f32),
            pltpu.VMEM((2, count, ROWS, cx), f32),
            pltpu.VMEM((2, count, ROWS, cz), f32),
            pltpu.VMEM((4, count, ROWS, LANES), f32),
            *[pltpu.VMEM((3, cz + 4 * ROWS, cx + LANES), f32)] * 3,
            pltpu.VMEM((total, cz, cx), bf16),
            pltpu.VMEM((total, cz, cx), bf16),
            pltpu.VMEM((cx, MODES), bf16),
            pltpu.VMEM((cx, MODES), bf16),
            pltpu.VMEM((chunks, y_n, units, cz, lanes), f32),
            pltpu.VMEM((chunks, y_n, units, cz, lanes), f32),
            pltpu.VMEM((chunks, y_n, units, cz, lanes), f32),
            pltpu.VMEM((chunks, others, units, cz, lanes), f32),
            pltpu.VMEM((chunks, others, units, cz, lanes), f32),
            pltpu.VMEM((chunks, units, cz, lanes), f32),
            pltpu.VMEM((chunks, z_n, cz, lanes), f32),
            pltpu.VMEM((chunks, z_n, cz, lanes), f32),
            dma((2,)),
            dma((chunks, y_n)),
            dma((chunks, y_n)),
            dma((chunks, others, units)),
            dma((chunks, others, units)),
            dma((chunks, units)),
            dma((chunks, z_n)),
            dma((chunks, z_n)),
            dma((chunks, total)),
            dma((chunks, others, units)),
            dma((chunks, y_n, units)),
            dma((8,)),
            dma((8,)),
        ],
        compiler_params=pltpu.CompilerParams(collective_id=0, has_side_effects=True),
        name="filter",
    )(velocity.reshape(count, cz, cx), slab, shear, mode_counts, txh, txl, *(jnp.asarray(t) for t in (tzh, tzl, tth, ttl)))
    stress = pl.pallas_call(
        synthesis_kernel,
        grid=(planes,),
        out_shape=jax.ShapeDtypeStruct((6, planes, cz, cx), f32),
        in_specs=[
            pl.BlockSpec((chunks, FIELDS, cz, lanes), lambda p: (0, p, 0, 0)), anywhere, anywhere
        ],
        out_specs=pl.BlockSpec((6, 1, cz, cx), lambda p: (0, p, 0, 0)),
        scratch_shapes=[pltpu.VMEM((cx, MODES), bf16), pltpu.VMEM((cx, MODES), bf16), dma((2,))],
        name="synthesis",
    )(gathered, txh, txl)
    return advanced.reshape(velocity.shape), stress


def local(sizes, velocity, slab, shear, mode_counts):
    return filtered_stress(velocity, slab, shear, mode_counts, sizes)


def solution(mesh):
    sizes = (mesh.shape["gx"], mesh.shape["gz"], mesh.shape["grp"])
    spread = P(None, None, ("gz", "grp"), "gx")
    return jax.shard_map(
        functools.partial(local, sizes),
        mesh=mesh,
        in_specs=(spread, P(), P(), P()),
        out_specs=(spread, spread),
        check_vma=False,
    )
```

```python
import functools
import math

import jax
import jax.numpy as jnp
import numpy as np
from jax import lax
from jax.experimental import pallas as pl
from jax.experimental.pallas import tpu as pltpu
from jax.sharding import PartitionSpec as P

MODES = 256
FIELDS = 9
MESH = pl.DeviceIdType.MESH
ROWS = 8
LANES = 128

molecular_diffusivity = 0.4
time_step = 0.2
pair_first = (0, 0, 0, 1, 1, 2)
pair_second = (0, 1, 2, 1, 2, 2)
f32 = jnp.float32
bf16 = jnp.bfloat16


def wave_table(length):
    column = np.arange(MODES)
    half = MODES // 2
    numbers = np.where(column < half, column, column - half + 1)
    angles = (np.arange(length)[:, None] * numbers[None, :] % length) * (2.0 * math.pi / length)
    return np.where(column[None, :] < half, np.cos(angles), np.sin(angles)).astype(np.float32)


def split_table(table):
    high = table.astype(bf16)
    low = (table - high.astype(np.float32)).astype(bf16)
    return high, low


def split(values):
    high = values.astype(bf16)
    return high, (values - high.astype(f32)).astype(bf16)


def dot3(a, b, contract=((1,), (0,))):
    def one(x, y):
        return lax.dot_general(x, y, (contract, ((), ())), preferred_element_type=f32)

    return one(a[0], b[0]) + (one(a[0], b[1]) + one(a[1], b[0]))


def step_plane(p, planes, v_ref, zh_ref, xh_ref, corner_ref, slab, shear, out_ref, start, first, second):
    _, cz, cx = v_ref.shape
    top = 2 * ROWS
    lane = lax.broadcasted_iota(jnp.int32, (ROWS, LANES), 1)
    width = cx + LANES
    for c in range(3):
        start[c, top : top + cz, 0:cx] = v_ref[c * planes + p]
        strip = jnp.concatenate(
            [
                xh_ref[0, c * planes + p],
                jnp.zeros((LANES - 2 * ROWS, cz), f32),
                xh_ref[1, c * planes + p],
            ], axis=0
        )
        start[c, top : top + cz, cx:width] = strip.T
        for side, row in ((1, top - ROWS), (0, top + cz)):
            start[c, row : row + ROWS, 0:cx] = zh_ref[side, c * planes + p]
            start[c, row : row + ROWS, cx:width] = jnp.where(
                lane < LANES // 2,
                corner_ref[2 * side, c * planes + p],
                corner_ref[2 * side + 1, c * planes + p],
            )

    def block(source, row):
        middle = [source[c, row : row + ROWS, :] for c in range(3)]
        rates = []
        for c in range(3):
            north = source[c, row + 1 : row + 1 + ROWS, :]
            south = source[c, row - 1 : row - 1 + ROWS, :]
            east = pltpu.roll(middle[c], width - 1, 1)
            west = pltpu.roll(middle[c], 1, 1)
            value = (
                -(slab + middle[0]) * ((east - west) * 0.5)
                - middle[2] * ((north - south) * 0.5)
                + molecular_diffusivity * (east + west + north + south - 4.0 * middle[c])
            )
            rates.append(value - shear * middle[1] if c == 0 else value)
        return middle, rates

    for row in range(ROWS, top + cz + ROWS, ROWS):
        middle, rates = block(start, row)
        for c in range(3):
            first[c, row : row + ROWS, :] = middle[c] + time_step * rates[c]
    for row in range(ROWS, top + cz + ROWS, ROWS):
        middle, rates = block(first, row)
        for c in range(3):
            second[c, row : row + ROWS, :] = 0.75 * start[c, row : row + ROWS, :] + 0.25 * (
                middle[c] + time_step * rates[c]
            )
    for row in range(top, top + cz, ROWS):
        middle, rates = block(second, row)
        for c in range(3):
            value = start[c, row : row + ROWS, :] * (1.0 / 3.0) + (2.0 / 3.0) * (
                middle[c] + time_step * rates[c]
            )
            out_ref[c * planes + p, row - top : row - top + ROWS, :] = value[:, 0:cx]


def filter_kernel(
    sizes, planes, v_ref, slab_ref, shear_ref, counts_ref, txh_hbm, txl_hbm, tzh_ref, tzl_ref, tth_ref,
    ttl_ref, gath, adv_ref, strips, zh_ref, xh_ref, corner_ref, start, first_ref, second_ref,
    high, low, txh, txl, part_send, part_keep, part_recv, y_send, y_recv, z_send, z_recv, z_out,
    table_sem, ps_sem, pr_sem, ys_sem, yr_sem, zs_sem, zr_sem, os_sem, gr_sem, gy_sem, gp_sem,
    hs_sem, hr_sem,
):
    gx_n, gz_n, grp_n = sizes
    z_n = gz_n * grp_n
    y_n = gx_n // 2
    chunks, total_units, _, lanes = gath.shape
    units = total_units // gx_n
    count, cz, cx = adv_ref.shape
    gx = lax.axis_index("gx")
    z = lax.axis_index("gz") * grp_n + lax.axis_index("grp")
    y, core = lax.div(gx, 2), lax.rem(gx, 2)
    other = 1 - core

    def at_x(to_y, to_core):
        return {"gx": 2 * to_y + to_core, "gz": lax.axis_index("gz"), "grp": lax.axis_index("grp")}

    def at_z(to_z):
        to_z = jnp.int32(to_z)
        return {"gx": gx, "gz": lax.div(to_z, grp_n), "grp": lax.rem(to_z, grp_n)}

    def remote(src, dst, send, recv, device):
        return pltpu.make_async_remote_copy(
            src_ref=src, dst_ref=dst, send_sem=send, recv_sem=recv, device_id=device, device_id_type=MESH
        )

    barrier = pltpu.get_barrier_semaphore()
    friends = [at_x(y, other)]
    friends += [at_x(lax.rem(y + d, y_n), core) for d in range(1, y_n)]
    friends += [at_z(lax.rem(z + d, z_n)) for d in range(1, z_n)]
    steps = [(dx, dz) for dx in (-1, 0, 1) for dz in (-1, 0, 1) if dx or dz]

    def near(dx, dz):
        to_z = lax.rem(z + dz + z_n, z_n)
        return {
            "gx": lax.rem(gx + dx + gx_n, gx_n),
            "gz": lax.div(to_z, grp_n),
            "grp": lax.rem(to_z, grp_n),
        }

    friends += [near(dx, dz) for dx, dz in steps]
    for friend in friends:
        pl.semaphore_signal(barrier, inc=1, device_id=friend, device_id_type=MESH)

    mine = pl.ds(pl.multiple_of(gx * cx, cx), cx)
    tables = [
        pltpu.make_async_copy(txh_hbm.at[mine, :], txh, table_sem.at[0]),
        pltpu.make_async_copy(txl_hbm.at[mine, :], txl, table_sem.at[1]),
    ]
    for copy in tables:
        copy.start()

    for c in range(count):
        strips[0, c] = v_ref[c, :, 0:LANES].T[0:ROWS]
        strips[1, c] = v_ref[c, :, cx - LANES : cx].T[LANES - ROWS : LANES]
    pl.semaphore_wait(barrier, len(friends))
    edge_x = {1: pl.ds(cx - LANES, LANES), -1: pl.ds(0, LANES), 0: pl.ds(0, cx)}
    edge_z = {1: pl.ds(cz - ROWS, ROWS), -1: pl.ds(0, ROWS)}
    edges = []
    for index, (dx, dz) in enumerate(steps):
        side_x, side_z = int(dx > 0), int(dz > 0)
        if dz == 0:
            source, target = strips.at[side_x], xh_ref.at[side_x]
        else:
            source = v_ref.at[:, edge_z[dz], edge_x[dx]]
            target = zh_ref.at[side_z] if dx == 0 else corner_ref.at[2 * side_z + side_x]
        edges.append(remote(source, target, hs_sem.at[index], hr_sem.at[index], near(dx, dz)))
    for copy in edges:
        copy.start()
    for copy in edges:
        copy.wait()

    def put(unit, values):
        h, l = split(values)
        high[unit] = h
        low[unit] = l

    def prepare(p, carry):
        step_plane(
            p, planes, v_ref, zh_ref, xh_ref, corner_ref, slab_ref[p], shear_ref[p], adv_ref, start,
            first_ref, second_ref,
        )
        parts = [adv_ref[i * planes + p] for i in range(3)]
        for i in range(3):
            put(p * FIELDS + i, parts[i])
        for q, (a, b) in enumerate(zip(pair_first, pair_second)):
            put(p * FIELDS + 3 + q, parts[a] * parts[b])
        return carry

    lax.fori_loop(0, planes, prepare, 0)
    for unit in range(planes * FIELDS, total_units):
        high[unit] = jnp.zeros((cz, cx), bf16)
        low[unit] = jnp.zeros((cz, cx), bf16)
    for copy in tables:
        copy.wait()

    def analyse(block, target, d):
        chosen = pl.ds(block * units, units)
        rows = (high[chosen].reshape(units * cz, cx), low[chosen].reshape(units * cz, cx))
        sums = dot3(rows, (txh[...], txl[...]))
        for h in range(chunks):
            target[h, d] = sums[:, h * lanes : (h + 1) * lanes].reshape(units, cz, lanes)

    def to_partner(h, d):
        return remote(
            part_send.at[h, d], part_recv.at[h, d], ps_sem.at[h, d], pr_sem.at[h, d], at_x(y, other)
        )

    def to_y(h, d, k):
        return remote(
            y_send.at[h, d - 1, k], y_recv.at[h, d - 1, k], ys_sem.at[h, d - 1, k], yr_sem.at[h, d - 1, k],
            at_x(lax.rem(y + d, y_n), core),
        )

    turns = [lax.rem(z + i, units) for i in range(units)]

    def send_y(h, d, k):
        y_send[h, d - 1, k] = part_keep[h, d, k] + part_recv[h, d, k]
        to_y(h, d, k).start()

    def forward(h, k):
        return remote(z_send.at[h, k], z_recv.at[h, z], zs_sem.at[h, k], zr_sem.at[h, z], at_z(k))

    unit = gx * units + z

    def back(h, s, slot):
        return remote(z_out.at[h, s], gath.at[h, slot], os_sem.at[h, s], gr_sem.at[h, slot], at_z(s))

    def send_z(h):
        to_partner(h, 0).wait_recv()
        for d in range(1, y_n):
            if h + 1 < chunks:
                to_partner(h + 1, d).wait_recv()
        for k in turns:
            for d in range(1, y_n):
                to_y(h, d, k).wait_recv()
                if h + 1 < chunks:
                    send_y(h + 1, d, k)
            total = part_keep[h, 0, k] + part_recv[h, 0, k]
            for d in range(1, y_n):
                total = total + y_recv[h, d - 1, k]
            z_send[h, k] = total

            @pl.when(z != k)
            def _():
                forward(h, k).start()

            @pl.when(z == k)
            def _():
                z_recv[h, z] = total

    def filter_lines(h):
        for s in range(z_n):

            @pl.when(z != s)
            def _():
                remote(
                    z_send.at[h, 0], z_recv.at[h, s], zs_sem.at[h, 0], zr_sem.at[h, s], at_z(s)
                ).wait_recv()

        plane = jnp.minimum(lax.div(unit, FIELDS), planes - 1)
        limit_x, limit_z = counts_ref[plane, 0], counts_ref[plane, 1]

        def numbers(axis, start):
            column = lax.broadcasted_iota(jnp.int32, (MODES, lanes), axis) + start
            half = MODES // 2
            return jnp.where(column < half, column, column - half + 1), column

        def weights(column, length):
            return jnp.where(column == 0, f32(1.0 / length), f32(2.0 / length))

        kz, nz = numbers(0, 0)
        kx, nx = numbers(1, h * lanes)
        scale = weights(nz, z_n * cz) * weights(nx, gx_n * cx)
        scale = jnp.where((kz <= limit_z) & (kx <= limit_x), scale, 0.0)
        lines = split(z_recv[h].reshape(z_n * cz, lanes))
        spectral = dot3((tth_ref[...], ttl_ref[...]), lines) * scale
        z_out[h] = dot3((tzh_ref[...], tzl_ref[...]), split(spectral)).reshape(z_n, cz, lanes)
        for s in range(z_n):

            @pl.when(z != s)
            def _():
                back(h, s, unit).start()

            @pl.when(z == s)
            def _():
                gath[h, unit] = z_out[h, s]

    def spread(h, slot, k, d):
        return remote(
            gath.at[h, slot], gath.at[h, slot], gy_sem.at[h, d - 1, k], gr_sem.at[h, slot],
            at_x(lax.rem(y + d, y_n), core),
        )

    def share(h, slot, d, k):
        return remote(
            gath.at[h, slot], gath.at[h, slot], gp_sem.at[h, d, k], gr_sem.at[h, slot], at_x(y, other)
        )

    def spread_own(h):
        for k in range(units):
            slot = gx * units + k

            @pl.when(z != k)
            def _():
                back(h, 0, slot).wait_recv()

            for d in range(1, y_n):
                spread(h, slot, k, d).start()
            share(h, slot, 0, k).start()

    def share_others(h):
        for d in range(1, y_n):
            for k in range(units):
                slot = (2 * lax.rem(y + d, y_n) + core) * units + k
                back(h, 0, slot).wait_recv()
                share(h, slot, d, k).start()

    order = list(range(1, y_n)) + [0]
    for d in order:
        analyse(2 * lax.rem(y + d, y_n) + other, part_send, d)
        for h in range(chunks):
            to_partner(h, d).start()
        analyse(2 * lax.rem(y + d, y_n) + core, part_keep, d)
        if d:
            to_partner(0, d).wait_recv()
            for k in turns:
                send_y(0, d, k)
    send_z(0)

    @pl.when(z < units)
    def _():
        filter_lines(0)

    for h in range(1, chunks):
        send_z(h)
    for h in range(chunks):
        spread_own(h)
        if h + 1 < chunks:

            @pl.when(z < units)
            def _():
                filter_lines(h + 1)

        share_others(h)
    for h in range(chunks):
        for d in range(y_n):
            for k in range(units):
                back(h, 0, (2 * lax.rem(y + d, y_n) + other) * units + k).wait_recv()

    for h in range(chunks):
        for d in range(y_n):
            to_partner(h, d).wait_send()
        for d in range(1, y_n):
            for k in range(units):
                to_y(h, d, k).wait_send()
        for k in range(units):

            @pl.when(z != k)
            def _():
                forward(h, k).wait_send()

            for d in range(1, y_n):
                spread(h, gx * units + k, k, d).wait_send()
            for d in range(y_n):
                share(h, gx * units + k, d, k).wait_send()

        @pl.when(z < units)
        def _():
            for s in range(z_n):

                @pl.when(z != s)
                def _():
                    back(h, s, unit).wait_send()


def synthesis_kernel(gath_ref, txh_hbm, txl_hbm, out_ref, txh, txl, table_sem):
    chunks, _, cz, _ = gath_ref.shape
    cx = txh.shape[0]

    @pl.when(pl.program_id(0) == 0)
    def _():
        mine = pl.ds(pl.multiple_of(lax.axis_index("gx") * cx, cx), cx)
        copies = [
            pltpu.make_async_copy(txh_hbm.at[mine, :], txh, table_sem.at[0]),
            pltpu.make_async_copy(txl_hbm.at[mine, :], txl, table_sem.at[1]),
        ]
        for copy in copies:
            copy.start()
        for copy in copies:
            copy.wait()

    rows = jnp.concatenate([gath_ref[h].reshape(FIELDS * cz, -1) for h in range(chunks)], axis=1)
    filtered = dot3(split(rows), (txh[...], txl[...]), ((1,), (1,))).reshape(FIELDS, cz, cx)
    for q, (a, b) in enumerate(zip(pair_first, pair_second)):
        out_ref[q, 0] = filtered[3 + q] - filtered[a] * filtered[b]


def filtered_stress(velocity, slab, shear, mode_counts, sizes):
    gx_n, gz_n, grp_n = sizes
    z_n = gz_n * grp_n
    y_n = gx_n // 2
    three, planes, cz, cx = velocity.shape
    count = three * planes
    units = -(-FIELDS * planes // gx_n)
    assert gx_n % 2 == 0 and units <= z_n
    txh, txl = (jnp.asarray(t) for t in split_table(wave_table(cx * gx_n)))
    table_z = wave_table(cz * z_n)
    tzh, tzl = split_table(table_z)
    tth, ttl = split_table(table_z.T)
    dma = pltpu.SemaphoreType.DMA
    vmem = pl.BlockSpec(memory_space=pltpu.VMEM)
    anywhere = pl.BlockSpec(memory_space=pl.ANY)
    others = max(y_n - 1, 1)
    total = gx_n * units
    chunks = 2
    lanes = MODES // chunks
    smem = pl.BlockSpec(memory_space=pltpu.SMEM)
    gathered, advanced = pl.pallas_call(
        functools.partial(filter_kernel, sizes, planes),
        out_shape=(
            jax.ShapeDtypeStruct((chunks, total, cz, lanes), f32),
            jax.ShapeDtypeStruct((count, cz, cx), f32),
        ),
        in_specs=[vmem, smem, smem, smem, anywhere, anywhere, vmem, vmem, vmem, vmem],
        out_specs=(vmem, vmem),
        scratch_shapes=[
            pltpu.VMEM((2, count, ROWS, cz), f32),
            pltpu.VMEM((2, count, ROWS, cx), f32),
            pltpu.VMEM((2, count, ROWS, cz), f32),
            pltpu.VMEM((4, count, ROWS, LANES), f32),
            *[pltpu.VMEM((3, cz + 4 * ROWS, cx + LANES), f32)] * 3,
            pltpu.VMEM((total, cz, cx), bf16),
            pltpu.VMEM((total, cz, cx), bf16),
            pltpu.VMEM((cx, MODES), bf16),
            pltpu.VMEM((cx, MODES), bf16),
            pltpu.VMEM((chunks, y_n, units, cz, lanes), f32),
            pltpu.VMEM((chunks, y_n, units, cz, lanes), f32),
            pltpu.VMEM((chunks, y_n, units, cz, lanes), f32),
            pltpu.VMEM((chunks, others, units, cz, lanes), f32),
            pltpu.VMEM((chunks, others, units, cz, lanes), f32),
            pltpu.VMEM((chunks, units, cz, lanes), f32),
            pltpu.VMEM((chunks, z_n, cz, lanes), f32),
            pltpu.VMEM((chunks, z_n, cz, lanes), f32),
            dma((2,)),
            dma((chunks, y_n)),
            dma((chunks, y_n)),
            dma((chunks, others, units)),
            dma((chunks, others, units)),
            dma((chunks, units)),
            dma((chunks, z_n)),
            dma((chunks, z_n)),
            dma((chunks, total)),
            dma((chunks, others, units)),
            dma((chunks, y_n, units)),
            dma((8,)),
            dma((8,)),
        ],
        compiler_params=pltpu.CompilerParams(collective_id=0, has_side_effects=True),
        name="filter",
    )(velocity.reshape(count, cz, cx), slab, shear, mode_counts, txh, txl, *(jnp.asarray(t) for t in (tzh, tzl, tth, ttl)))
    stress = pl.pallas_call(
        synthesis_kernel,
        grid=(planes,),
        out_shape=jax.ShapeDtypeStruct((6, planes, cz, cx), f32),
        in_specs=[
            pl.BlockSpec((chunks, FIELDS, cz, lanes), lambda p: (0, p, 0, 0)), anywhere, anywhere
        ],
        out_specs=pl.BlockSpec((6, 1, cz, cx), lambda p: (0, p, 0, 0)),
        scratch_shapes=[pltpu.VMEM((cx, MODES), bf16), pltpu.VMEM((cx, MODES), bf16), dma((2,))],
        name="synthesis",
    )(gathered, txh, txl)
    return advanced.reshape(velocity.shape), stress


def local(sizes, velocity, slab, shear, mode_counts):
    return filtered_stress(velocity, slab, shear, mode_counts, sizes)


def solution(mesh):
    sizes = (mesh.shape["gx"], mesh.shape["gz"], mesh.shape["grp"])
    spread = P(None, None, ("gz", "grp"), "gx")
    return jax.shard_map(
        functools.partial(local, sizes),
        mesh=mesh,
        in_specs=(spread, P(), P(), P()),
        out_specs=(spread, spread),
        check_vma=False,
    )
```
